256 devices in a mesh: ctx: 32 (over x_lo, z, core), tp: 8 (over y, x_hi).
Axes of the slice: x: 4 (x_hi: 2, x_lo: 2; x = x_hi * 2 + x_lo), y: 4, z: 8, core: 2. Of those that a mesh axis runs over, the one named last changes fastest.
Arguments:
- q_in: float32 [16384, 2048], P('ctx', 'tp'), may hold values from -6 to 6
- k_in: float32 [16384, 2048], P('ctx', 'tp'), may hold values from -6 to 6
- v_in: float32 [16384, 2048], P('ctx', 'tp'), may hold values from -6 to 6
- short_taps: float32 [3, 3, 2048], P(None, None, 'tp'), may hold values from -3.5 to 3.5
- long_filter: float32 [16384, 2048], P('ctx', 'tp'), may hold values from -6 to 6
- skip_gain: float32 [2048], P('tp'), may hold values from 0.5 to 1.5
- conv_saved: float32 [16384, 2048], P('ctx', 'tp'), may hold values from -6 to 6
- grad_out: float32 [16384, 2048], P('ctx', 'tp'), may hold values from -6 to 6
Outputs:
- grad_q: float32 [16384, 2048], P('ctx', 'tp')
- grad_k: float32 [16384, 2048], P('ctx', 'tp')
- grad_v: float32 [16384, 2048], P('ctx', 'tp')
- grad_filter: float32 [2048, 16384], P(('ctx', 'tp'))
- grad_taps: float32 [3, 3, 2048], P(None, None, 'tp')
- grad_skip: float32 [2048], P('tp')
The draws below stay inside these ranges and needn't reach their ends.
All inputs are finite; a program needn't handle non-finite values.
Results may differ from the reference program's by a relative error of at most 0.00018.
Values sent between devices are 32-bit elements; how exact they have to be, the bound alone decides.
No kernel may reach another device: no remote copies, remote signals or barrier semaphores. Data moves between devices by JAX's collectives and lax.ppermute only.
A program may use at most 128 MiB of HBM per device.

```python
import math
import jax
import jax.numpy as jnp
from jax import lax

C = 2048
SEQ = 16384


def block_scale(rng, shape, cuts, smallest, top_value):
    def one(dim, parts):
        steps = jax.random.uniform(jax.random.fold_in(jax.random.fold_in(rng, 6), dim), (parts,), jnp.float32, smallest / len(cuts), top_value / len(cuts))
        return jnp.repeat(jnp.exp(steps), shape[dim] // parts).reshape((-1,) + (1,) * (len(shape) - dim - 1))

    factor_of = one(*cuts[0])
    for cut in cuts[1:]:
        factor_of = factor_of * one(*cut)
    return factor_of


def noise(stream_key, extent, deviation, bound, shards=(), held_as=jnp.bfloat16):
    values = deviation * jax.random.normal(stream_key, extent, jnp.float32)
    if shards:
        values = values * block_scale(stream_key, extent, shards, -0.22, 0.18)
    return jnp.clip(values, -bound, bound).astype(held_as)


def setup_inputs(seed: int = 0) -> dict:
    keys = jax.random.split(jax.random.key(seed), 9)
    q_in = noise(keys[0], (SEQ, C), 1.0, 6.0, ((0, 32), (1, 8)), jnp.float32)
    k_in = noise(keys[1], (SEQ, C), 1.0, 6.0, ((0, 32), (1, 8)), jnp.float32)
    v_in = noise(keys[2], (SEQ, C), 1.0, 6.0, ((0, 32), (1, 8)), jnp.float32)
    short_taps = noise(keys[3], (3, 3, C), 3 ** -0.5, 3.5, ((2, 8),), jnp.float32)
    long_filter = noise(keys[4], (SEQ, C), 1.0, 6.0, ((0, 32), (1, 8)), jnp.float32)
    skip_gain = jnp.clip(0.5 + 1.0 * jax.random.uniform(keys[5], (C,), jnp.float32) ** block_scale(keys[5], (C,), ((0, 8),), -0.2, 0.2), 0.5, 1.5)
    conv_saved = noise(keys[6], (SEQ, C), 1.0, 6.0, ((0, 32), (1, 8)), jnp.float32)
    grad_out = noise(keys[7], (SEQ, C), 1.0, 6.0, ((0, 32), (1, 8)), jnp.float32)
    return {"q_in": q_in, "k_in": k_in, "v_in": v_in, "short_taps": short_taps, "long_filter": long_filter, "skip_gain": skip_gain, "conv_saved": conv_saved, "grad_out": grad_out}


def shorten(signal, weights):
    length = signal.shape[0]
    padded = jnp.pad(signal, ((2, 0), (0, 0)))
    return weights[0] * padded[2:] + weights[1] * padded[1:length + 1] + weights[2] * padded[:length]

def lengthen(grads, weights):
    length = grads.shape[0]
    padded = jnp.pad(grads, ((0, 2), (0, 0)))
    return weights[0] * padded[:length] + weights[1] * padded[1:length + 1] + weights[2] * padded[2:]

def tap_sums(grads, signal):
    length = signal.shape[0]
    padded = jnp.pad(signal, ((2, 0), (0, 0)))
    return jnp.stack([lax.optimization_barrier(jnp.sum(grads * padded[2 - offset:2 - offset + length], axis=0)) for offset in range(3)])

def correlate_block(pieces):
    filter_block, grad_block, zeta_block = pieces
    padded_length = 2 * SEQ
    spec_filter = jnp.fft.rfft(filter_block, n=padded_length, axis=0)
    spec_grad = jnp.fft.rfft(grad_block, n=padded_length, axis=0)
    spec_zeta = jnp.fft.rfft(zeta_block, n=padded_length, axis=0)
    corr_filter = jnp.fft.irfft(jnp.conj(spec_filter) * spec_grad, n=padded_length, axis=0)[:SEQ]
    corr_zeta = jnp.fft.irfft(jnp.conj(spec_zeta) * spec_grad, n=padded_length, axis=0)[:SEQ]
    return (corr_filter, corr_zeta)

def reference(q_in, k_in, v_in, short_taps, long_filter, skip_gain, conv_saved, grad_out):
    q_short = shorten(q_in, short_taps[0])
    k_short = shorten(k_in, short_taps[1])
    v_short = shorten(v_in, short_taps[2])
    product_kv = k_short * v_short
    grad_w = grad_out * q_short
    grad_qs = grad_out * conv_saved
    block_width = math.gcd(C, 256)
    block_count = C // block_width

    def to_blocks(array):
        return jnp.transpose(array.reshape(SEQ, block_count, block_width), (1, 0, 2))

    def from_blocks(array):
        return jnp.transpose(array, (1, 0, 2)).reshape(SEQ, C)
    corr_filter, corr_zeta = lax.map(correlate_block, (to_blocks(long_filter), to_blocks(grad_w), to_blocks(product_kv)))
    corr_filter = from_blocks(corr_filter)
    corr_zeta = from_blocks(corr_zeta)
    filter_scale = 1.0 / math.sqrt(SEQ)
    grad_z = skip_gain * grad_w + filter_scale * corr_filter
    grad_ks = grad_z * v_short
    grad_vs = grad_z * k_short
    grad_q = lengthen(grad_qs, short_taps[0])
    grad_k = lengthen(grad_ks, short_taps[1])
    grad_v = lengthen(grad_vs, short_taps[2])
    grad_taps = jnp.stack([tap_sums(grad_qs, q_in), tap_sums(grad_ks, k_in), tap_sums(grad_vs, v_in)])
    grad_skip = lax.optimization_barrier(jnp.sum(grad_w * product_kv, axis=0))
    grad_filter = jnp.transpose(filter_scale * corr_zeta)
    return (grad_q, grad_k, grad_v, grad_filter, grad_taps, grad_skip)
```

```python
import functools
import math

import jax
import jax.numpy as jnp
import numpy as np
from jax import lax
from jax.experimental import pallas as pl
from jax.experimental.pallas import tpu as pltpu
from jax.sharding import PartitionSpec as P


f32, bf16 = jnp.float32, jnp.bfloat16
LANES = 128


def tp_target(c, t):
    x_lo, zp, k = c >> 4, (c >> 2) & 3, c & 3
    return ((x_lo ^ (t >> 2) ^ (k & 1)) << 2) | ((t - zp - k) & 3)


def owner_of(group, t):
    k, target = group // 8, group % 8
    zp = (t - target - k) & 3
    x_lo = (target >> 2) ^ (t >> 2) ^ (k & 1)
    return x_lo * 16 + zp * 4 + k


def halves(table):
    table = np.asarray(table, np.float64).astype(np.float32)
    high = table.astype(bf16)
    low = (table - high.astype(np.float32)).astype(bf16)
    return high, low


@functools.cache
def tables(blocks, scale):
    total = 2 * blocks * 4 * LANES
    rows = np.arange(4 * blocks)
    a = (rows % blocks) * 4 + rows // blocks
    q = np.arange(LANES) + 0.5
    l = np.arange(LANES)
    ang = 2 * np.pi * np.outer(q, a) / (total // LANES)
    outer = np.concatenate([np.cos(ang), -np.sin(ang)], 0)
    back = scale * np.concatenate([np.cos(ang), -np.sin(ang)], 0).T
    ang = 2 * np.pi * np.outer(q, l) / total
    twist_re, twist_im = np.cos(ang).astype(np.float32), -np.sin(ang).astype(np.float32)
    ang = 2 * np.pi * (np.outer(l, l) % LANES) / LANES
    co, si = np.cos(ang), np.sin(ang)
    inner = np.block([[co, -si], [si, co]])
    inner_back = np.block([[co, si], [-si, co]])
    oh, ol = halves(outer)
    bh, bl = halves(back)
    ih, il = halves(inner)
    jh, jl = halves(inner_back)
    return (np.concatenate([oh, oh], 1), ol, twist_re, twist_im, ih, il, jh, jl, bh, bl)


def split(x):
    high = x.astype(bf16)
    return high, (x - high.astype(f32)).astype(bf16)


def mm(a, b):
    return jnp.dot(a, b, preferred_element_type=f32)


def load_pair(src, row_a, row_b, stride, blocks):
    def one(row):
        return jnp.concatenate(
            [src[pl.ds(i * stride + row, blocks, stride=4 * stride), :] for i in range(4)],
            axis=0,
        )

    return jnp.concatenate([one(row_a), one(row_b)], axis=1)


def forward(pair, oh, ol, tr, ti, ih, il):
    high, low = split(pair)
    y = mm(oh[...], jnp.concatenate([high, low], axis=0)) + mm(ol[...], high)
    re, im = tr[...], ti[...]
    parts = []
    for s in (0, LANES):
        yr, yi = y[:LANES, s : s + LANES], y[LANES:, s : s + LANES]
        parts.append(jnp.concatenate([yr * re - yi * im, yr * im + yi * re], axis=1))
    high, low = split(jnp.concatenate(parts, axis=0))
    return mm(high, ih[...]) + mm(low, ih[...]) + mm(high, il[...])


def conj_times(f, g):
    fr, fi, gr, gi = f[:, :LANES], f[:, LANES:], g[:, :LANES], g[:, LANES:]
    return jnp.concatenate([fr * gr + fi * gi, fr * gi - fi * gr], axis=1)


def backward(pa, pb, tr, ti, jh, jl, bh, bl):
    high, low = split(jnp.concatenate([pa, pb], axis=0))
    v = mm(high, jh[...]) + mm(low, jh[...]) + mm(high, jl[...])
    re, im = tr[...], ti[...]
    parts = []
    for s in (0, LANES):
        vr, vi = v[s : s + LANES, :LANES], v[s : s + LANES, LANES:]
        parts.append(jnp.concatenate([vr * re + vi * im, vi * re - vr * im], axis=0))
    high, low = split(jnp.concatenate(parts, axis=1))
    return mm(bh[...], high) + mm(bh[...], low) + mm(bl[...], high)


def first_kernel(blocks, src, oh, ol, tr, ti, ih, il, jh, jl, bh, bl, out, spec):
    for ch in range(0, 8, 2):
        products = []
        for c in (ch, ch + 1):
            both = forward(load_pair(src, c, 8 + c, 24, blocks), oh, ol, tr, ti, ih, il)
            spec[c] = both[LANES:]
            products.append(conj_times(both[:LANES], both[LANES:]))
        corr = backward(*products, tr, ti, jh, jl, bh, bl)
        for s in (0, 1):
            for i in range(4):
                out[pl.ds(i * 8 + ch + s, blocks, stride=32), :] = corr[
                    i * blocks : (i + 1) * blocks, s * LANES : (s + 1) * LANES
                ]


def second_kernel(blocks, src, spec, oh, ol, tr, ti, ih, il, jh, jl, bh, bl, out, held):
    for ch in range(0, 8, 2):
        both = forward(load_pair(src, 16 + ch, 17 + ch, 24, blocks), oh, ol, tr, ti, ih, il)
        products = [
            conj_times(both[:LANES], spec[ch]),
            conj_times(both[LANES:], spec[ch + 1]),
        ]
        corr = backward(*products, tr, ti, jh, jl, bh, bl)
        for s in (0, 1):
            for i in range(4):
                held[pl.ds(i * 8 + ch + s, blocks, stride=32), :] = corr[
                    i * blocks : (i + 1) * blocks, s * LANES : (s + 1) * LANES
                ]
    for a in range(4 * blocks):
        out[:, a * LANES : (a + 1) * LANES] = held[a * 8 : (a + 1) * 8, :]


def put_ext(ext, i, prev, x):
    ext[i, 6:8, :] = prev[i]
    ext[i, 8:, :] = x[...]


def shorted(ext, i, taps, r0, n):
    return (
        taps[i, 0:1, :] * ext[i, 8 + r0 : 8 + r0 + n, :]
        + taps[i, 1:2, :] * ext[i, 7 + r0 : 7 + r0 + n, :]
        + taps[i, 2:3, :] * ext[i, 6 + r0 : 6 + r0 + n, :]
    )


def send_kernel(t_ref, taps, prev, q, k, v, go, fil, out, ext):
    t = t_ref[0]
    for i, x in enumerate((q, k, v)):
        put_ext(ext, i, prev, x)
    groups = out.shape[0]
    owners = [owner_of(g, t) for g in range(groups)]
    for r0 in range(0, q.shape[0], LANES):
        gw = go[r0 : r0 + LANES, :] * shorted(ext, 0, taps, r0, LANES)
        kv = shorted(ext, 1, taps, r0, LANES) * shorted(ext, 2, taps, r0, LANES)
        for i, piece in enumerate((fil[r0 : r0 + LANES, :], gw, kv)):
            turned = jnp.transpose(piece)
            for g in range(groups):
                out[owners[g], r0 // LANES, i * 8 : i * 8 + 8, :] = turned[g * 8 : g * 8 + 8]


def side_kernel(
    taps, prev, q, k, v, go, cs, gain, following, zbase, ks, vs, gq, sums, ext, gext
):
    n = q.shape[0]
    for i, x in enumerate((q, k, v)):
        put_ext(ext, i, prev, x)
    gext[n : n + 2, :] = following[...]
    for r0 in range(0, n, LANES):
        gext[r0 : r0 + LANES, :] = go[r0 : r0 + LANES, :] * cs[r0 : r0 + LANES, :]
    totals = [jnp.zeros((1, q.shape[1]), f32) for _ in range(4)]
    for r0 in range(0, n, LANES):
        rows = slice(r0, r0 + LANES)
        gw = go[rows, :] * shorted(ext, 0, taps, r0, LANES)
        k_short = shorted(ext, 1, taps, r0, LANES)
        v_short = shorted(ext, 2, taps, r0, LANES)
        zbase[rows, :] = gain[...] * gw
        ks[rows, :] = k_short
        vs[rows, :] = v_short
        g = gext[rows, :]
        gq[rows, :] = (
            taps[0, 0:1, :] * g
            + taps[0, 1:2, :] * gext[r0 + 1 : r0 + 1 + LANES, :]
            + taps[0, 2:3, :] * gext[r0 + 2 : r0 + 2 + LANES, :]
        )
        for o in range(3):
            totals[o] += jnp.sum(
                g * ext[0, 8 + r0 - o : 8 + r0 - o + LANES, :], axis=0, keepdims=True
            )
        totals[3] += jnp.sum(gw * (k_short * v_short), axis=0, keepdims=True)
    for o in range(4):
        sums[o : o + 1, :] = totals[o]
    sums[4:, :] = jnp.zeros((4, q.shape[1]), f32)


def last_kernel(t_ref, corr, zbase, ks, vs, taps, prev, k, v, gk, gv, heads, sums, ext, gext, held):
    t = t_ref[0]
    n = k.shape[0]
    groups = corr.shape[0]
    owners = [owner_of(g, t) for g in range(groups)]
    for i, x in enumerate((k, v)):
        ext[i, 6:8, :] = prev[i + 1]
        ext[i, 8:, :] = x[...]
        gext[i, n:, :] = jnp.zeros((8, k.shape[1]), f32)
    totals = [jnp.zeros((1, k.shape[1]), f32) for _ in range(6)]
    for r0 in range(0, n, LANES):
        rows = slice(r0, r0 + LANES)
        for g in range(groups):
            held[g * 8 : g * 8 + 8, :] = corr[owners[g], r0 // LANES]
        grad_z = zbase[rows, :] + jnp.transpose(held[...])
        for i, other in enumerate((vs, ks)):
            g = grad_z * other[rows, :]
            gext[i, rows, :] = g
            for o in range(3):
                totals[i * 3 + o] += jnp.sum(
                    g * ext[i, 8 + r0 - o : 8 + r0 - o + LANES, :], axis=0, keepdims=True
                )
    for o in range(6):
        sums[o : o + 1, :] = totals[o]
    sums[6:, :] = jnp.zeros((2, k.shape[1]), f32)
    for i, out in enumerate((gk, gv)):
        heads[i] = gext[i, 0:2, :]
        for r0 in range(0, n, LANES):
            out[r0 : r0 + LANES, :] = (
                taps[i + 1, 0:1, :] * gext[i, r0 : r0 + LANES, :]
                + taps[i + 1, 1:2, :] * gext[i, r0 + 1 : r0 + 1 + LANES, :]
                + taps[i + 1, 2:3, :] * gext[i, r0 + 2 : r0 + 2 + LANES, :]
            )


def seam_kernel(gk_in, gv_in, nxt, taps, gk, gv):
    for i, (src, dst) in enumerate(((gk_in, gk), (gv_in, gv))):
        one, two = taps[i + 1, 1:2, :], taps[i + 1, 2:3, :]
        first, second = nxt[i, 0:1, :], nxt[i, 1:2, :]
        dst[...] = src[...]
        dst[6:7, :] = src[6:7, :] + two * first
        dst[7:8, :] = src[7:8, :] + one * first + two * second


VM = pl.BlockSpec(memory_space=pltpu.VMEM)
SM = pl.BlockSpec(memory_space=pltpu.SMEM)


def shape(*s):
    return jax.ShapeDtypeStruct(s, f32)


def call(body, ins, outs, args, scratch=(), name=None, flops=10**6, nbytes=4 * 10**6):
    return pl.pallas_call(
        body,
        out_shape=outs,
        in_specs=ins,
        out_specs=jax.tree.map(lambda _: VM, outs),
        scratch_shapes=list(scratch),
        name=name,
        cost_estimate=pl.CostEstimate(flops=flops, bytes_accessed=nbytes, transcendentals=0),
        compiler_params=pltpu.CompilerParams(vmem_limit_bytes=40 * 2**20),
    )(*args)


def shifted(value, steps):
    count = lax.axis_size("ctx")
    pairs = [(i, i + steps) for i in range(count) if 0 <= i + steps < count]
    return lax.ppermute(value, "ctx", pairs)


def summed(x):
    def flips(y, masks):
        parts = [lax.ppermute(y, "ctx", [(i, i ^ m) for i in range(32)]) for m in masks]
        for p in parts:
            y = y + p
        return y

    return flips(flips(x, (1, 16, 17)), tuple(range(2, 16, 2)))


def on_device(q, k, v, taps, fil, gain, cs, go):
    n, width = q.shape
    blocks = lax.axis_size("ctx")
    tp = lax.axis_size("tp")
    seq = n * blocks
    scale = 2.0 / (2 * seq) / math.sqrt(seq)
    tabs = [jnp.asarray(x) for x in tables(blocks, scale)]
    t = lax.axis_index("tp").astype(jnp.int32).reshape(1)

    prev = shifted(jnp.stack([q[n - 2 :], k[n - 2 :], v[n - 2 :]]), 1)
    nxt_q = shifted(go[:2] * cs[:2], -1)

    ext3 = pltpu.VMEM((3, n + 8, width), f32)
    packed = call(
        send_kernel, [SM] + [VM] * 7, shape(blocks, n // LANES, 24, LANES),
        (t, taps, prev, q, k, v, go, fil), [ext3], "send",
    )
    arrived = lax.all_to_all(packed, "ctx", 0, 0, tiled=True).reshape(-1, LANES)
    zbase, ks, vs, gq, sums_q = call(
        side_kernel, [VM] * 9,
        (shape(n, width),) * 4 + (shape(8, width),),
        (taps, prev, q, k, v, go, cs, gain.reshape(1, width), nxt_q),
        [ext3, pltpu.VMEM((n + 8, width), f32)], "side",
    )
    corr, spec = call(
        functools.partial(first_kernel, blocks), [VM] * 11,
        (shape(seq * 8 // LANES, LANES), shape(8, LANES, 2 * LANES)),
        (arrived, *tabs), name="first", flops=2 * 10**9,
    )
    back = lax.all_to_all(corr.reshape(blocks, n // LANES, 8, LANES), "ctx", 0, 0, tiled=True)
    zeta = call(
        functools.partial(second_kernel, blocks), [VM] * 12,
        shape(8, seq), (arrived, spec, *tabs),
        [pltpu.VMEM((seq * 8 // LANES, LANES), f32)], "second", flops=2 * 10**9,
    )
    hop_one, hop_two = [], []
    for c in range(blocks):
        for s in range(tp):
            target = tp_target(c, s)
            hop_one.append((c * tp + s, c * tp + target))
            hop_two.append((c * tp + target, (4 * s + c % 4) * tp + target))
    zeta = lax.ppermute(zeta, ("ctx", "tp"), hop_one)
    grad_filter = lax.ppermute(zeta, ("ctx", "tp"), hop_two)

    gk, gv, heads, sums_kv = call(
        last_kernel, [SM] + [VM] * 8,
        (shape(n, width), shape(n, width), shape(2, 2, width), shape(8, width)),
        (t, back, zbase, ks, vs, taps, prev, k, v),
        [
            pltpu.VMEM((2, n + 8, width), f32),
            pltpu.VMEM((2, n + 8, width), f32),
            pltpu.VMEM((width, LANES), f32),
        ], "last",
    )
    nxt = shifted(heads, -1)
    edge = pl.BlockSpec((8, width), lambda i: (n // 8 - 1, 0))
    gk, gv = pl.pallas_call(
        seam_kernel,
        grid=(1,),
        out_shape=(shape(n, width), shape(n, width)),
        in_specs=[edge, edge, VM, VM],
        out_specs=(edge, edge),
        input_output_aliases={0: 0, 1: 1},
        name="seam",
    )(gk, gv, nxt, taps)
    total = summed(jnp.concatenate([sums_q[:4], sums_kv[:6], sums_q[4:], sums_kv[6:8]]))
    grad_taps = jnp.concatenate([total[0:3], total[4:10]]).reshape(3, 3, width)
    return gq, gk, gv, grad_filter, grad_taps, total[3]


def solution(mesh):
    rows = P("ctx", "tp")
    return jax.shard_map(
        on_device,
        mesh=mesh,
        in_specs=(rows, rows, rows, P(None, None, "tp"), rows, P("tp"), rows, rows),
        out_specs=(rows, rows, rows, P(("ctx", "tp"), None), P(None, None, "tp"), P("tp")),
        check_vma=False,
    )
```

```python
import functools
import math

import jax
import jax.numpy as jnp
import numpy as np
from jax import lax
from jax.experimental import pallas as pl
from jax.experimental.pallas import tpu as pltpu
from jax.sharding import PartitionSpec as P


f32, bf16 = jnp.float32, jnp.bfloat16
LANES = 128


def target_of(c, t):
    x_lo, zp, par, core = c >> 4, (c >> 2) & 3, (c >> 1) & 1, c & 1
    ahead = (t - zp) & 3
    far, kind = ahead >> 1, ahead & 1
    spread = far ^ core ^ (par if kind else 0)
    new_par = far if kind else par ^ far
    across = (t >> 2) ^ x_lo ^ core
    return 4 * t + 2 * new_par + core, across * 4 + kind * 2 + spread


def owner_of(group, t):
    new_par, core, target = group >> 4, (group >> 3) & 1, group & 7
    across, kind, spread = target >> 2, (target >> 1) & 1, target & 1
    far = new_par if kind else spread ^ core
    par = far ^ core ^ spread if kind else new_par ^ far
    zp = (t - (2 * far + kind)) & 3
    x_lo = (t >> 2) ^ across ^ core
    return x_lo * 16 + zp * 4 + par * 2 + core


def halves(table):
    table = np.asarray(table, np.float64).astype(np.float32)
    high = table.astype(bf16)
    low = (table - high.astype(np.float32)).astype(bf16)
    return high, low


@functools.cache
def tables(blocks, scale):
    total = 2 * blocks * 4 * LANES
    rows = np.arange(4 * blocks)
    a = (rows % blocks) * 4 + rows // blocks
    q = np.arange(LANES) + 0.5
    l = np.arange(LANES)
    ang = 2 * np.pi * np.outer(q, a) / (total // LANES)
    outer = np.concatenate([np.cos(ang), -np.sin(ang)], 0)
    back = scale * np.concatenate([np.cos(ang), -np.sin(ang)], 0).T
    ang = 2 * np.pi * np.outer(q, l) / total
    twist_re, twist_im = np.cos(ang).astype(np.float32), -np.sin(ang).astype(np.float32)
    ang = 2 * np.pi * (np.outer(l, l) % LANES) / LANES
    co, si = np.cos(ang), np.sin(ang)
    inner = np.block([[co, -si], [si, co]])
    inner_back = np.block([[co, si], [-si, co]])
    oh, ol = halves(outer)
    bh, bl = halves(back)
    ih, il = halves(inner)
    jh, jl = halves(inner_back)
    ol = np.concatenate([ol[:LANES], ol[LANES:]], 1)
    big = np.concatenate([np.concatenate([oh, oh], 1), ih, il, jh, jl, bh, bl, ol], 0)
    return big, np.concatenate([twist_re, twist_im], 0)


def split(x):
    high = x.astype(bf16)
    return high, (x - high.astype(f32)).astype(bf16)


def mm(a, b):
    return jnp.dot(a, b, preferred_element_type=f32)


def load_pair(src, row_a, row_b, stride, blocks):
    def one(row):
        return jnp.concatenate(
            [src[pl.ds(i * stride + row, blocks, stride=4 * stride), :] for i in range(4)],
            axis=0,
        )

    return jnp.concatenate([one(row_a), one(row_b)], axis=1)


def forward(pair, tab, twist):
    high, low = split(pair)
    ol = jnp.concatenate([tab[1536:1664, :LANES], tab[1536:1664, LANES:]], axis=0)
    y = mm(tab[0:256, :], jnp.concatenate([high, low], axis=0)) + mm(ol, high)
    re, im = twist[:LANES, :], twist[LANES:, :]
    parts = []
    for s in (0, LANES):
        yr, yi = y[:LANES, s : s + LANES], y[LANES:, s : s + LANES]
        parts.append(jnp.concatenate([yr * re - yi * im, yr * im + yi * re], axis=1))
    high, low = split(jnp.concatenate(parts, axis=0))
    ih, il = tab[256:512, :], tab[512:768, :]
    return mm(high, ih) + mm(low, ih) + mm(high, il)


def conj_times(f, g):
    fr, fi, gr, gi = f[:, :LANES], f[:, LANES:], g[:, :LANES], g[:, LANES:]
    return jnp.concatenate([fr * gr + fi * gi, fr * gi - fi * gr], axis=1)


def backward(pa, pb, tab, twist):
    high, low = split(jnp.concatenate([pa, pb], axis=0))
    jh, jl = tab[768:1024, :], tab[1024:1280, :]
    v = mm(high, jh) + mm(low, jh) + mm(high, jl)
    re, im = twist[:LANES, :], twist[LANES:, :]
    parts = []
    for s in (0, LANES):
        vr, vi = v[s : s + LANES, :LANES], v[s : s + LANES, LANES:]
        parts.append(jnp.concatenate([vr * re + vi * im, vi * re - vr * im], axis=0))
    high, low = split(jnp.concatenate(parts, axis=1))
    bh, bl = tab[1280:1408, :], tab[1408:1536, :]
    return mm(bh, high) + mm(bh, low) + mm(bl, high)


def correlate(blocks, first, src, tab, twist, out):
    for ch in range(0, 8, 2):
        products = []
        for c in (ch, ch + 1):
            both = forward(load_pair(src, first + c, 8 + c, 24, blocks), tab, twist)
            products.append(conj_times(both[:LANES], both[LANES:]))
        corr = backward(*products, tab, twist)
        for s in (0, 1):
            for i in range(4):
                out[pl.ds(i * 8 + ch + s, blocks, stride=32), :] = corr[
                    i * blocks : (i + 1) * blocks, s * LANES : (s + 1) * LANES
                ]


def first_kernel(blocks, src, tab, twist, ahead, out):
    correlate(blocks, 0, src, tab, twist, out)


def second_kernel(blocks, src, tab, twist, out, held):
    correlate(blocks, 16, src, tab, twist, held)
    for a in range(4 * blocks):
        out[:, a * LANES : (a + 1) * LANES] = held[a * 8 : (a + 1) * 8, :]


def put_ext(ext, i, prev, x):
    ext[i, 6:8, :] = prev[2 * i : 2 * i + 2, :]
    ext[i, 8:, :] = x[...]


def shorted(ext, i, taps, r0, n):
    return (
        taps[i, 0:1, :] * ext[i, 8 + r0 : 8 + r0 + n, :]
        + taps[i, 1:2, :] * ext[i, 7 + r0 : 7 + r0 + n, :]
        + taps[i, 2:3, :] * ext[i, 6 + r0 : 6 + r0 + n, :]
    )


def edge_kernel(q, k, v, go, cs, tails, heads):
    for i, x in enumerate((q, k, v)):
        tails[2 * i : 2 * i + 2, :] = x[6:8, :]
    tails[6:8, :] = jnp.zeros((2, q.shape[1]), f32)
    heads[...] = go[...] * cs[...]


def send_kernel(t_ref, taps, prev, q, k, v, go, fil, out, ext, gof, sems):
    n = q.shape[0]
    copies = [
        pltpu.make_async_copy(src, dst, sems.at[i])
        for i, (src, dst) in enumerate(
            (
                (fil, gof.at[0]),
                (k, ext.at[1, pl.ds(8, n)]),
                (v, ext.at[2, pl.ds(8, n)]),
                (q, ext.at[0, pl.ds(8, n)]),
                (go, gof.at[1]),
            )
        )
    ]
    for c in copies:
        c.start()
    t = t_ref[0]
    for i in range(3):
        ext[i, 6:8, :] = prev[2 * i : 2 * i + 2, :]
    groups = out.shape[0]
    owners = [owner_of(g, t) for g in range(groups)]

    def put(i, r0, piece):
        turned = jnp.transpose(piece)
        for g in range(groups):
            out[owners[g], r0 // LANES, i * 8 : i * 8 + 8, :] = turned[g * 8 : g * 8 + 8]

    starts = range(0, n, LANES)
    copies[0].wait()
    for r0 in starts:
        put(0, r0, gof[0, r0 : r0 + LANES, :])
    copies[1].wait()
    copies[2].wait()
    for r0 in starts:
        put(2, r0, shorted(ext, 1, taps, r0, LANES) * shorted(ext, 2, taps, r0, LANES))
    copies[3].wait()
    copies[4].wait()
    for r0 in starts:
        put(1, r0, gof[1, r0 : r0 + LANES, :] * shorted(ext, 0, taps, r0, LANES))


def side_kernel(
    taps, prev, q, k, v, go, cs, gain, following, zbase, ks, vs, gq, sums, ext, gext
):
    n = q.shape[0]
    for i, x in enumerate((q, k, v)):
        put_ext(ext, i, prev, x)
    gext[n : n + 8, :] = following[...]
    for r0 in range(0, n, LANES):
        gext[r0 : r0 + LANES, :] = go[r0 : r0 + LANES, :] * cs[r0 : r0 + LANES, :]
    totals = [jnp.zeros((1, q.shape[1]), f32) for _ in range(4)]
    for r0 in range(0, n, LANES):
        rows = slice(r0, r0 + LANES)
        gw = go[rows, :] * shorted(ext, 0, taps, r0, LANES)
        k_short = shorted(ext, 1, taps, r0, LANES)
        v_short = shorted(ext, 2, taps, r0, LANES)
        zbase[rows, :] = gain[...] * gw
        ks[rows, :] = k_short
        vs[rows, :] = v_short
        g = gext[rows, :]
        gq[rows, :] = (
            taps[0, 0:1, :] * g
            + taps[0, 1:2, :] * gext[r0 + 1 : r0 + 1 + LANES, :]
            + taps[0, 2:3, :] * gext[r0 + 2 : r0 + 2 + LANES, :]
        )
        for o in range(3):
            totals[o] += jnp.sum(
                g * ext[0, 8 + r0 - o : 8 + r0 - o + LANES, :], axis=0, keepdims=True
            )
        totals[3] += jnp.sum(gw * (k_short * v_short), axis=0, keepdims=True)
    for o in range(4):
        sums[o : o + 1, :] = totals[o]
    sums[4:, :] = jnp.zeros((4, q.shape[1]), f32)


def last_kernel(t_ref, corr, zbase, ks, vs, taps, prev, k, v, gk, gv, heads, sums, ext, gext, held):
    t = t_ref[0]
    n = k.shape[0]
    groups = corr.shape[0]
    owners = [owner_of(g, t) for g in range(groups)]
    for i, x in enumerate((k, v)):
        ext[i, 6:8, :] = prev[2 * i + 2 : 2 * i + 4, :]
        ext[i, 8:, :] = x[...]
        gext[i, n:, :] = jnp.zeros((8, k.shape[1]), f32)
    totals = [jnp.zeros((1, k.shape[1]), f32) for _ in range(6)]
    for r0 in range(0, n, LANES):
        rows = slice(r0, r0 + LANES)
        for g in range(groups):
            held[g * 8 : g * 8 + 8, :] = corr[owners[g], r0 // LANES]
        grad_z = zbase[rows, :] + jnp.transpose(held[...])
        for i, other in enumerate((vs, ks)):
            g = grad_z * other[rows, :]
            gext[i, rows, :] = g
            for o in range(3):
                totals[i * 3 + o] += jnp.sum(
                    g * ext[i, 8 + r0 - o : 8 + r0 - o + LANES, :], axis=0, keepdims=True
                )
    width = k.shape[1]
    for o in range(6):
        part = jnp.broadcast_to(totals[o].reshape(1, 1, width), (groups, 1, width))
        sums[:, :, o * width : (o + 1) * width] = part
    for i, out in enumerate((gk, gv)):
        heads[i] = gext[i, 0:2, :]
        for r0 in range(0, n, LANES):
            out[r0 : r0 + LANES, :] = (
                taps[i + 1, 0:1, :] * gext[i, r0 : r0 + LANES, :]
                + taps[i + 1, 1:2, :] * gext[i, r0 + 1 : r0 + 1 + LANES, :]
                + taps[i + 1, 2:3, :] * gext[i, r0 + 2 : r0 + 2 + LANES, :]
            )


def seam_kernel(gk_in, gv_in, nxt, taps, gk, gv):
    for i, (src, dst) in enumerate(((gk_in, gk), (gv_in, gv))):
        one, two = taps[i + 1, 1:2, :], taps[i + 1, 2:3, :]
        first, second = nxt[i, 0:1, :], nxt[i, 1:2, :]
        dst[...] = src[...]
        dst[6:7, :] = src[6:7, :] + two * first
        dst[7:8, :] = src[7:8, :] + one * first + two * second


def finish_kernel(parts, early, taps, skip):
    width = skip.shape[1]
    total = parts[0]
    for i in range(1, parts.shape[0]):
        total = total + parts[i]
    taps[0] = early[0:3, :]
    for i in range(2):
        for o in range(3):
            at = (3 * i + o) * width
            taps[i + 1, o : o + 1, :] = total[:, at : at + width]
    skip[...] = early[3:4, :]


VM = pl.BlockSpec(memory_space=pltpu.VMEM)
SM = pl.BlockSpec(memory_space=pltpu.SMEM)
HB = pl.BlockSpec(memory_space=pl.ANY)


def shape(*s):
    return jax.ShapeDtypeStruct(s, f32)


def call(body, ins, outs, args, scratch=(), name=None, flops=10**6, nbytes=4 * 10**6):
    return pl.pallas_call(
        body,
        out_shape=outs,
        in_specs=ins,
        out_specs=jax.tree.map(lambda _: VM, outs),
        scratch_shapes=list(scratch),
        name=name,
        cost_estimate=pl.CostEstimate(flops=flops, bytes_accessed=nbytes, transcendentals=0),
        compiler_params=pltpu.CompilerParams(vmem_limit_bytes=40 * 2**20),
    )(*args)


def shifted(value, steps):
    count = lax.axis_size("ctx")
    pairs = [(i, i + steps) for i in range(count) if 0 <= i + steps < count]
    return lax.ppermute(value, "ctx", pairs)


def on_device(q, k, v, taps, fil, gain, cs, go):
    n, width = q.shape
    blocks = lax.axis_size("ctx")
    tp = lax.axis_size("tp")
    seq = n * blocks
    scale = 2.0 / (2 * seq) / math.sqrt(seq)
    tabs = [jnp.asarray(x) for x in tables(blocks, scale)]
    t = lax.axis_index("tp").astype(jnp.int32).reshape(1)

    low = pl.BlockSpec((8, width), lambda i: (n // 8 - 1, 0))
    top = pl.BlockSpec((8, width), lambda i: (0, 0))
    tails, heads = pl.pallas_call(
        edge_kernel,
        grid=(1,),
        out_shape=(shape(8, width), shape(8, width)),
        in_specs=[low, low, low, top, top],
        out_specs=(top, top),
        name="edge",
    )(q, k, v, go, cs)
    prev = shifted(tails, 1)
    nxt_q = shifted(heads, -1)

    ext3 = pltpu.VMEM((3, n + 8, width), f32)
    packed = call(
        send_kernel, [SM, VM, VM] + [HB] * 5, shape(blocks, n // LANES, 24, LANES),
        (t, taps, prev, q, k, v, go, fil),
        [ext3, pltpu.VMEM((2, n, width), f32), pltpu.SemaphoreType.DMA((5,))], "send",
    )
    arrived = lax.all_to_all(packed, "ctx", 0, 0, tiled=True).reshape(-1, LANES)
    zbase, ks, vs, gq, early = call(
        side_kernel, [VM] * 9,
        (shape(n, width),) * 4 + (shape(8, width),),
        (taps, prev, q, k, v, go, cs, gain.reshape(1, width), nxt_q),
        [ext3, pltpu.VMEM((n + 8, width), f32)], "side",
    )
    for mask in (1, 16, 2, 4, 8):
        early = early + lax.ppermute(early, "ctx", [(i, i ^ mask) for i in range(blocks)])
    corr = call(
        functools.partial(first_kernel, blocks), [VM] * 3 + [HB],
        shape(seq * 8 // LANES, LANES), (arrived, *tabs, early), name="first",
        flops=2 * 10**9,
    )
    back = lax.all_to_all(corr.reshape(blocks, n // LANES, 8, LANES), "ctx", 0, 0, tiled=True)
    zeta = call(
        functools.partial(second_kernel, blocks), [VM] * 3,
        shape(8, seq), (arrived, *tabs),
        [pltpu.VMEM((seq * 8 // LANES, LANES), f32)], "second", flops=2 * 10**9,
    )
    hop_one, hop_two = [], []
    for c in range(blocks):
        for s in range(tp):
            row, column = target_of(c, s)
            hop_one.append((c * tp + s, c * tp + column))
            hop_two.append((c * tp + column, row * tp + column))
    zeta = lax.ppermute(zeta, ("ctx", "tp"), hop_one)
    grad_filter = lax.ppermute(zeta, ("ctx", "tp"), hop_two)

    gk, gv, heads, parts = call(
        last_kernel, [SM] + [VM] * 8,
        (shape(n, width), shape(n, width), shape(2, 2, width), shape(blocks, 1, 6 * width)),
        (t, back, zbase, ks, vs, taps, prev, k, v),
        [
            pltpu.VMEM((2, n + 8, width), f32),
            pltpu.VMEM((2, n + 8, width), f32),
            pltpu.VMEM((width, LANES), f32),
        ], "last",
    )
    parts = lax.all_to_all(parts, "ctx", 0, 0, tiled=True)
    nxt = shifted(heads, -1)
    gk, gv = pl.pallas_call(
        seam_kernel,
        grid=(1,),
        out_shape=(shape(n, width), shape(n, width)),
        in_specs=[low, low, VM, VM],
        out_specs=(low, low),
        input_output_aliases={0: 0, 1: 1},
        name="seam",
    )(gk, gv, nxt, taps)
    grad_taps, grad_skip = call(
        finish_kernel, [VM, VM], (shape(3, 3, width), shape(1, width)), (parts, early),
        name="finish",
    )
    return gq, gk, gv, grad_filter, grad_taps, grad_skip.reshape(width)


def solution(mesh):
    rows = P("ctx", "tp")
    return jax.shard_map(
        on_device,
        mesh=mesh,
        in_specs=(rows, rows, rows, P(None, None, "tp"), rows, P("tp"), rows, rows),
        out_specs=(rows, rows, rows, P(("ctx", "tp"), None), P(None, None, "tp"), P("tp")),
        check_vma=False,
    )
```

```python
import functools
import math

import jax
import jax.numpy as jnp
import numpy as np
from jax import lax
from jax.experimental import pallas as pl
from jax.experimental.pallas import tpu as pltpu
from jax.sharding import PartitionSpec as P


f32, bf16 = jnp.float32, jnp.bfloat16
LANES = 128


def target_of(c, t):
    x_lo, zp, par, core = c >> 4, (c >> 2) & 3, (c >> 1) & 1, c & 1
    ahead = (t - zp) & 3
    far, kind = ahead >> 1, ahead & 1
    spread = far ^ core ^ (par if kind else 0)
    new_par = far if kind else par ^ far
    across = (t >> 2) ^ x_lo ^ core
    return 4 * t + 2 * new_par + core, across * 4 + kind * 2 + spread


def owner_of(group, t):
    new_par, core, target = group >> 4, (group >> 3) & 1, group & 7
    across, kind, spread = target >> 2, (target >> 1) & 1, target & 1
    far = new_par if kind else spread ^ core
    par = far ^ core ^ spread if kind else new_par ^ far
    zp = (t - (2 * far + kind)) & 3
    x_lo = (t >> 2) ^ across ^ core
    return x_lo * 16 + zp * 4 + par * 2 + core


def halves(table):
    table = np.asarray(table, np.float64).astype(np.float32)
    high = table.astype(bf16)
    low = (table - high.astype(np.float32)).astype(bf16)
    return high, low


@functools.cache
def tables(blocks, scale):
    total = 2 * blocks * 4 * LANES
    rows = np.arange(4 * blocks)
    a = (rows % blocks) * 4 + rows // blocks
    q = np.arange(LANES) + 0.5
    l = np.arange(LANES)
    ang = 2 * np.pi * np.outer(q, a) / (total // LANES)
    outer = np.concatenate([np.cos(ang), -np.sin(ang)], 0)
    back = scale * np.concatenate([np.cos(ang), -np.sin(ang)], 0).T
    ang = 2 * np.pi * np.outer(q, l) / total
    twist_re, twist_im = np.cos(ang).astype(np.float32), -np.sin(ang).astype(np.float32)
    ang = 2 * np.pi * (np.outer(l, l) % LANES) / LANES
    co, si = np.cos(ang), np.sin(ang)
    inner = np.block([[co, -si], [si, co]])
    inner_back = np.block([[co, si], [-si, co]])
    oh, ol = halves(outer)
    bh, bl = halves(back)
    ih, il = halves(inner)
    jh, jl = halves(inner_back)
    ol = np.concatenate([ol[:LANES], ol[LANES:]], 1)
    big = np.concatenate([np.concatenate([oh, oh], 1), ih, il, jh, jl, bh, bl, ol], 0)
    return big, np.concatenate([twist_re, twist_im], 0)


def split(x):
    high = x.astype(bf16)
    return high, (x - high.astype(f32)).astype(bf16)


def mm(a, b):
    return jnp.dot(a, b, preferred_element_type=f32)


def load_pair(src_a, src_b, row_a, row_b, blocks):
    def one(src, row):
        return jnp.concatenate(
            [src[pl.ds(i * 8 + row, blocks, stride=32), :] for i in range(4)], axis=0
        )

    return jnp.concatenate([one(src_a, row_a), one(src_b, row_b)], axis=1)


def forward(pair, tab, twist):
    high, low = split(pair)
    ol = jnp.concatenate([tab[1536:1664, :LANES], tab[1536:1664, LANES:]], axis=0)
    y = mm(tab[0:256, :], jnp.concatenate([high, low], axis=0)) + mm(ol, high)
    re, im = twist[:LANES, :], twist[LANES:, :]
    parts = []
    for s in (0, LANES):
        yr, yi = y[:LANES, s : s + LANES], y[LANES:, s : s + LANES]
        parts.append(jnp.concatenate([yr * re - yi * im, yr * im + yi * re], axis=1))
    high, low = split(jnp.concatenate(parts, axis=0))
    ih, il = tab[256:512, :], tab[512:768, :]
    return mm(high, ih) + mm(low, ih) + mm(high, il)


def conj_times(f, g):
    fr, fi, gr, gi = f[:, :LANES], f[:, LANES:], g[:, :LANES], g[:, LANES:]
    return jnp.concatenate([fr * gr + fi * gi, fr * gi - fi * gr], axis=1)


def backward(pa, pb, tab, twist):
    high, low = split(jnp.concatenate([pa, pb], axis=0))
    jh, jl = tab[768:1024, :], tab[1024:1280, :]
    v = mm(high, jh) + mm(low, jh) + mm(high, jl)
    re, im = twist[:LANES, :], twist[LANES:, :]
    parts = []
    for s in (0, LANES):
        vr, vi = v[s : s + LANES, :LANES], v[s : s + LANES, LANES:]
        parts.append(jnp.concatenate([vr * re + vi * im, vi * re - vr * im], axis=0))
    high, low = split(jnp.concatenate(parts, axis=1))
    bh, bl = tab[1280:1408, :], tab[1408:1536, :]
    return mm(bh, high) + mm(bh, low) + mm(bl, high)


def correlate(blocks, which, src, tab_in, twist_in, out, left, right, tab, twist, sems):
    pairs = (
        (src.at[:, pl.ds(8 * which, 8)], left),
        (src.at[:, pl.ds(8, 8)], right),
        (tab_in, tab),
        (twist_in, twist),
    )
    copies = [pltpu.make_async_copy(x, y, sems.at[i]) for i, (x, y) in enumerate(pairs)]
    for c in copies:
        c.start()
    for c in copies:
        c.wait()
    left, right = (x.reshape(32 * blocks, LANES) for x in (left, right))
    for ch in range(0, 8, 2):
        products = []
        for c in (ch, ch + 1):
            both = forward(load_pair(left, right, c, c, blocks), tab, twist)
            products.append(conj_times(both[:LANES], both[LANES:]))
        corr = backward(*products, tab, twist)
        for s in (0, 1):
            for i in range(4):
                out[pl.ds(i * 8 + ch + s, blocks, stride=32), :] = corr[
                    i * blocks : (i + 1) * blocks, s * LANES : (s + 1) * LANES
                ]


def first_kernel(blocks, src, tab, twist, ahead, out, *scratch):
    correlate(blocks, 0, src, tab, twist, out, *scratch)


def second_kernel(blocks, src, tab, twist, out, held, *scratch):
    correlate(blocks, 2, src, tab, twist, held, *scratch)
    for a in range(4 * blocks):
        out[:, a * LANES : (a + 1) * LANES] = held[a * 8 : (a + 1) * 8, :]


def put_ext(ext, i, prev, x):
    ext[i, 6:8, :] = prev[2 * i : 2 * i + 2, :]
    ext[i, 8:, :] = x[...]


def shorted(ext, i, taps, r0, n):
    return (
        taps[i, 0:1, :] * ext[i, 8 + r0 : 8 + r0 + n, :]
        + taps[i, 1:2, :] * ext[i, 7 + r0 : 7 + r0 + n, :]
        + taps[i, 2:3, :] * ext[i, 6 + r0 : 6 + r0 + n, :]
    )


def edge_kernel(q, k, v, go, cs, tails, heads):
    for i, x in enumerate((q, k, v)):
        tails[2 * i : 2 * i + 2, :] = x[6:8, :]
    tails[6:8, :] = jnp.zeros((2, q.shape[1]), f32)
    heads[...] = go[...] * cs[...]


def send_kernel(t_ref, taps, prev, q, k, v, go, fil, ahead, out, ext, gof, sems):
    n = q.shape[0]
    copies = [
        pltpu.make_async_copy(src, dst, sems.at[i])
        for i, (src, dst) in enumerate(
            (
                (fil, gof.at[0]),
                (k, ext.at[1, pl.ds(8, n)]),
                (v, ext.at[2, pl.ds(8, n)]),
                (q, ext.at[0, pl.ds(8, n)]),
                (go, gof.at[1]),
            )
        )
    ]
    for c in copies:
        c.start()
    t = t_ref[0]
    for i in range(3):
        ext[i, 6:8, :] = prev[2 * i : 2 * i + 2, :]
    groups = out.shape[0]
    owners = [owner_of(g, t) for g in range(groups)]

    def put(i, r0, piece):
        turned = jnp.transpose(piece)
        for g in range(groups):
            out[owners[g], r0 // LANES, i * 8 : i * 8 + 8, :] = turned[g * 8 : g * 8 + 8]

    starts = range(0, n, LANES)
    copies[0].wait()
    for r0 in starts:
        put(0, r0, gof[0, r0 : r0 + LANES, :])
    copies[1].wait()
    copies[2].wait()
    for r0 in starts:
        put(2, r0, shorted(ext, 1, taps, r0, LANES) * shorted(ext, 2, taps, r0, LANES))
    copies[3].wait()
    copies[4].wait()
    for r0 in starts:
        put(1, r0, gof[1, r0 : r0 + LANES, :] * shorted(ext, 0, taps, r0, LANES))


def side_kernel(
    taps, prev, q, k, v, go, cs, gain, following, zbase, ks, vs, gq, sums, ext, gext
):
    n = q.shape[0]
    for i, x in enumerate((q, k, v)):
        put_ext(ext, i, prev, x)
    gext[n : n + 8, :] = following[...]
    for r0 in range(0, n, LANES):
        gext[r0 : r0 + LANES, :] = go[r0 : r0 + LANES, :] * cs[r0 : r0 + LANES, :]
    totals = [jnp.zeros((1, q.shape[1]), f32) for _ in range(4)]
    for r0 in range(0, n, LANES):
        rows = slice(r0, r0 + LANES)
        gw = go[rows, :] * shorted(ext, 0, taps, r0, LANES)
        k_short = shorted(ext, 1, taps, r0, LANES)
        v_short = shorted(ext, 2, taps, r0, LANES)
        zbase[rows, :] = gain[...] * gw
        ks[rows, :] = k_short
        vs[rows, :] = v_short
        g = gext[rows, :]
        gq[rows, :] = (
            taps[0, 0:1, :] * g
            + taps[0, 1:2, :] * gext[r0 + 1 : r0 + 1 + LANES, :]
            + taps[0, 2:3, :] * gext[r0 + 2 : r0 + 2 + LANES, :]
        )
        for o in range(3):
            totals[o] += jnp.sum(
                g * ext[0, 8 + r0 - o : 8 + r0 - o + LANES, :], axis=0, keepdims=True
            )
        totals[3] += jnp.sum(gw * (k_short * v_short), axis=0, keepdims=True)
    for o in range(4):
        sums[o : o + 1, :] = totals[o]
    sums[4:, :] = jnp.zeros((4, q.shape[1]), f32)


def last_kernel(t_ref, corr, zbase, ks, vs, taps, prev, k, v, early, gk, gv, heads, sums, ext, gext, held):
    t = t_ref[0]
    n = k.shape[0]
    groups = corr.shape[0]
    owners = [owner_of(g, t) for g in range(groups)]
    for i, x in enumerate((k, v)):
        ext[i, 6:8, :] = prev[2 * i + 2 : 2 * i + 4, :]
        ext[i, 8:, :] = x[...]
        gext[i, n:, :] = jnp.zeros((8, k.shape[1]), f32)
    totals = [jnp.zeros((1, k.shape[1]), f32) for _ in range(6)]
    for r0 in range(0, n, LANES):
        rows = slice(r0, r0 + LANES)
        for g in range(groups):
            held[g * 8 : g * 8 + 8, :] = corr[owners[g], r0 // LANES]
        grad_z = zbase[rows, :] + jnp.transpose(held[...])
        for i, other in enumerate((vs, ks)):
            g = grad_z * other[rows, :]
            gext[i, rows, :] = g
            for o in range(3):
                totals[i * 3 + o] += jnp.sum(
                    g * ext[i, 8 + r0 - o : 8 + r0 - o + LANES, :], axis=0, keepdims=True
                )
    width = k.shape[1]
    totals = [early[o : o + 1, :] for o in range(4)] + totals
    for o in range(10):
        part = jnp.broadcast_to(totals[o].reshape(1, 1, width), (groups, 1, width))
        sums[:, :, o * width : (o + 1) * width] = part
    for i, out in enumerate((gk, gv)):
        heads[i] = gext[i, 0:2, :]
        for r0 in range(0, n, LANES):
            out[r0 : r0 + LANES, :] = (
                taps[i + 1, 0:1, :] * gext[i, r0 : r0 + LANES, :]
                + taps[i + 1, 1:2, :] * gext[i, r0 + 1 : r0 + 1 + LANES, :]
                + taps[i + 1, 2:3, :] * gext[i, r0 + 2 : r0 + 2 + LANES, :]
            )


def seam_kernel(gk_in, gv_in, nxt, taps, gk, gv):
    for i, (src, dst) in enumerate(((gk_in, gk), (gv_in, gv))):
        one, two = taps[i + 1, 1:2, :], taps[i + 1, 2:3, :]
        first, second = nxt[i, 0:1, :], nxt[i, 1:2, :]
        dst[...] = src[...]
        dst[6:7, :] = src[6:7, :] + two * first
        dst[7:8, :] = src[7:8, :] + one * first + two * second


def finish_kernel(parts, taps, skip):
    width = skip.shape[1]
    total = parts[0]
    for i in range(1, parts.shape[0]):
        total = total + parts[i]
    rows = [total[:, i * width : (i + 1) * width] for i in range(10)]
    skip[...] = rows.pop(3)
    for i in range(9):
        taps[i // 3, i % 3 : i % 3 + 1, :] = rows[i]


VM = pl.BlockSpec(memory_space=pltpu.VMEM)
SM = pl.BlockSpec(memory_space=pltpu.SMEM)
HB = pl.BlockSpec(memory_space=pl.ANY)


def shape(*s):
    return jax.ShapeDtypeStruct(s, f32)


def call(body, ins, outs, args, scratch=(), flops=10**6, nbytes=4 * 10**6):
    return pl.pallas_call(
        body,
        out_shape=outs,
        in_specs=ins,
        out_specs=jax.tree.map(lambda _: VM, outs),
        scratch_shapes=list(scratch),
        cost_estimate=pl.CostEstimate(flops=flops, bytes_accessed=nbytes, transcendentals=0),
        compiler_params=pltpu.CompilerParams(vmem_limit_bytes=40 * 2**20),
    )(*args)


def shifted(value, steps):
    count = lax.axis_size("ctx")
    pairs = [(i, i + steps) for i in range(count) if 0 <= i + steps < count]
    return lax.ppermute(value, "ctx", pairs)


def on_device(q, k, v, taps, fil, gain, cs, go):
    n, width = q.shape
    blocks = lax.axis_size("ctx")
    tp = lax.axis_size("tp")
    seq = n * blocks
    scale = 2.0 / (2 * seq) / math.sqrt(seq)
    tabs = [jnp.asarray(x) for x in tables(blocks, scale)]
    t = lax.axis_index("tp").astype(jnp.int32).reshape(1)

    low = pl.BlockSpec((8, width), lambda i: (n // 8 - 1, 0))
    top = pl.BlockSpec((8, width), lambda i: (0, 0))
    tails, heads = pl.pallas_call(
        edge_kernel,
        grid=(1,),
        out_shape=(shape(8, width), shape(8, width)),
        in_specs=[low, low, low, top, top],
        out_specs=(top, top),
        name="edge",
    )(q, k, v, go, cs)
    prev = shifted(tails, 1)
    nxt_q = shifted(heads, -1)

    ext3 = pltpu.VMEM((3, n + 8, width), f32)
    packed = call(
        send_kernel, [SM, VM, VM] + [HB] * 6, shape(blocks, n // LANES, 24, LANES),
        (t, taps, prev, q, k, v, go, fil, nxt_q),
        [ext3, pltpu.VMEM((2, n, width), f32), pltpu.SemaphoreType.DMA((5,))],
    )
    arrived = lax.all_to_all(packed, "ctx", 0, 0, tiled=True)
    arrived = arrived.reshape(seq // LANES, 24, LANES)
    work = [
        pltpu.VMEM((seq // LANES, 8, LANES), f32),
        pltpu.VMEM((seq // LANES, 8, LANES), f32),
        *(pltpu.VMEM(x.shape, x.dtype) for x in tabs),
        pltpu.SemaphoreType.DMA((4,)),
    ]
    zbase, ks, vs, gq, early = call(
        side_kernel, [VM] * 9,
        (shape(n, width),) * 4 + (shape(8, width),),
        (taps, prev, q, k, v, go, cs, gain.reshape(1, width), nxt_q),
        [ext3, pltpu.VMEM((n + 8, width), f32)],
    )
    corr = call(
        functools.partial(first_kernel, blocks), [HB] * 4,
        shape(seq * 8 // LANES, LANES), (arrived, *tabs, early), work,
        flops=2 * 10**9,
    )
    back = lax.all_to_all(corr.reshape(blocks, n // LANES, 8, LANES), "ctx", 0, 0, tiled=True)
    zeta = call(
        functools.partial(second_kernel, blocks), [HB] * 3,
        shape(8, seq), (arrived, *tabs),
        [pltpu.VMEM((seq * 8 // LANES, LANES), f32), *work], flops=2 * 10**9,
    )
    hop_one, hop_two = [], []
    for c in range(blocks):
        for s in range(tp):
            row, column = target_of(c, s)
            hop_one.append((c * tp + s, c * tp + column))
            hop_two.append((c * tp + column, row * tp + column))
    zeta = lax.ppermute(zeta, ("ctx", "tp"), hop_one)
    grad_filter = lax.ppermute(zeta, ("ctx", "tp"), hop_two)

    gk, gv, heads, parts = call(
        last_kernel, [SM] + [VM] * 9,
        (shape(n, width), shape(n, width), shape(2, 2, width), shape(blocks, 1, 10 * width)),
        (t, back, zbase, ks, vs, taps, prev, k, v, early),
        [
            pltpu.VMEM((2, n + 8, width), f32),
            pltpu.VMEM((2, n + 8, width), f32),
            pltpu.VMEM((width, LANES), f32),
        ],
    )
    parts = lax.all_to_all(parts, "ctx", 0, 0, tiled=True)
    nxt = shifted(heads, -1)
    gk, gv = pl.pallas_call(
        seam_kernel,
        grid=(1,),
        out_shape=(shape(n, width), shape(n, width)),
        in_specs=[low, low, VM, VM],
        out_specs=(low, low),
        input_output_aliases={0: 0, 1: 1},
        name="seam",
    )(gk, gv, nxt, taps)
    grad_taps, grad_skip = call(
        finish_kernel, [VM], (shape(3, 3, width), shape(1, width)), (parts,),
    )
    return gq, gk, gv, grad_filter, grad_taps, grad_skip.reshape(width)


def solution(mesh):
    rows = P("ctx", "tp")
    return jax.shard_map(
        on_device,
        mesh=mesh,
        in_specs=(rows, rows, rows, P(None, None, "tp"), rows, P("tp"), rows, rows),
        out_specs=(rows, rows, rows, P(("ctx", "tp"), None), P(None, None, "tp"), P("tp")),
        check_vma=False,
    )
```

```python
import functools
import math

import jax
import jax.numpy as jnp
import numpy as np
from jax import lax
from jax.experimental import pallas as pl
from jax.experimental.pallas import tpu as pltpu
from jax.sharding import PartitionSpec as P


f32, bf16 = jnp.float32, jnp.bfloat16
LANES = 128


def target_of(c, t):
    x_lo, zp, par, core = c >> 4, (c >> 2) & 3, (c >> 1) & 1, c & 1
    ahead = (t - zp) & 3
    far, kind = ahead >> 1, ahead & 1
    spread = far ^ core ^ (par if kind else 0)
    new_par = far if kind else par ^ far
    across = (t >> 2) ^ x_lo ^ core
    return 4 * t + 2 * new_par + core, across * 4 + kind * 2 + spread


def owner_of(group, t):
    new_par, core, target = group >> 4, (group >> 3) & 1, group & 7
    across, kind, spread = target >> 2, (target >> 1) & 1, target & 1
    far = new_par if kind else spread ^ core
    par = far ^ core ^ spread if kind else new_par ^ far
    zp = (t - (2 * far + kind)) & 3
    x_lo = (t >> 2) ^ across ^ core
    return x_lo * 16 + zp * 4 + par * 2 + core


def halves(table):
    table = np.asarray(table, np.float64).astype(np.float32)
    high = table.astype(bf16)
    low = (table - high.astype(np.float32)).astype(bf16)
    return high, low


@functools.cache
def tables(blocks, scale):
    total = 2 * blocks * 4 * LANES
    rows = np.arange(4 * blocks)
    a = (rows % blocks) * 4 + rows // blocks
    q = np.arange(LANES) + 0.5
    l = np.arange(LANES)
    ang = 2 * np.pi * np.outer(q, a) / (total // LANES)
    outer = np.concatenate([np.cos(ang), -np.sin(ang)], 0)
    back = scale * np.concatenate([np.cos(ang), -np.sin(ang)], 0).T
    ang = 2 * np.pi * np.outer(q, l) / total
    twist_re, twist_im = np.cos(ang).astype(np.float32), -np.sin(ang).astype(np.float32)
    ang = 2 * np.pi * (np.outer(l, l) % LANES) / LANES
    co, si = np.cos(ang), np.sin(ang)
    inner = np.block([[co, -si], [si, co]])
    inner_back = np.block([[co, si], [-si, co]])
    oh, ol = halves(outer)
    bh, bl = halves(back)
    ih, il = halves(inner)
    jh, jl = halves(inner_back)
    ol = np.concatenate([ol[:LANES], ol[LANES:]], 1)
    big = np.concatenate([np.concatenate([oh, oh], 1), ih, il, jh, jl, bh, bl, ol], 0)
    return big, np.concatenate([twist_re, twist_im], 0)


def split(x):
    high = x.astype(bf16)
    return high, (x - high.astype(f32)).astype(bf16)


def mm(a, b):
    return jnp.dot(a, b, preferred_element_type=f32)


def load_pair(src_a, src_b, row_a, row_b, blocks):
    def one(src, row):
        return jnp.concatenate(
            [src[pl.ds(i * 8 + row, blocks, stride=32), :] for i in range(4)], axis=0
        )

    return jnp.concatenate([one(src_a, row_a), one(src_b, row_b)], axis=1)


def forward(pair, tab, twist):
    high, low = split(pair)
    ol = jnp.concatenate([tab[1536:1664, :LANES], tab[1536:1664, LANES:]], axis=0)
    y = mm(tab[0:256, :], jnp.concatenate([high, low], axis=0)) + mm(ol, high)
    re, im = twist[:LANES, :], twist[LANES:, :]
    parts = []
    for s in (0, LANES):
        yr, yi = y[:LANES, s : s + LANES], y[LANES:, s : s + LANES]
        parts.append(jnp.concatenate([yr * re - yi * im, yr * im + yi * re], axis=1))
    high, low = split(jnp.concatenate(parts, axis=0))
    ih, il = tab[256:512, :], tab[512:768, :]
    return mm(high, ih) + mm(low, ih) + mm(high, il)


def conj_times(f, g):
    fr, fi, gr, gi = f[:, :LANES], f[:, LANES:], g[:, :LANES], g[:, LANES:]
    return jnp.concatenate([fr * gr + fi * gi, fr * gi - fi * gr], axis=1)


def backward(pa, pb, tab, twist):
    high, low = split(jnp.concatenate([pa, pb], axis=0))
    jh, jl = tab[768:1024, :], tab[1024:1280, :]
    v = mm(high, jh) + mm(low, jh) + mm(high, jl)
    re, im = twist[:LANES, :], twist[LANES:, :]
    parts = []
    for s in (0, LANES):
        vr, vi = v[s : s + LANES, :LANES], v[s : s + LANES, LANES:]
        parts.append(jnp.concatenate([vr * re + vi * im, vi * re - vr * im], axis=0))
    high, low = split(jnp.concatenate(parts, axis=1))
    bh, bl = tab[1280:1408, :], tab[1408:1536, :]
    return mm(bh, high) + mm(bh, low) + mm(bl, high)


def correlate(blocks, which, src, tab_in, twist_in, out, left, right, tab, twist, sems):
    pairs = (
        (src.at[:, pl.ds(8 * which, 8)], left),
        (src.at[:, pl.ds(8, 8)], right),
        (tab_in, tab),
        (twist_in, twist),
    )
    copies = [pltpu.make_async_copy(x, y, sems.at[i]) for i, (x, y) in enumerate(pairs)]
    for c in copies:
        c.start()
    for c in copies:
        c.wait()
    left, right = (x.reshape(32 * blocks, LANES) for x in (left, right))
    for ch in range(0, 8, 2):
        products = []
        for c in (ch, ch + 1):
            both = forward(load_pair(left, right, c, c, blocks), tab, twist)
            products.append(conj_times(both[:LANES], both[LANES:]))
        corr = backward(*products, tab, twist)
        for s in (0, 1):
            for i in range(4):
                out[pl.ds(i * 8 + ch + s, blocks, stride=32), :] = corr[
                    i * blocks : (i + 1) * blocks, s * LANES : (s + 1) * LANES
                ]


def first_kernel(blocks, src, tab, twist, ahead, out, *scratch):
    correlate(blocks, 0, src, tab, twist, out, *scratch)


def second_kernel(blocks, src, tab, twist, early, late, held, *scratch):
    correlate(blocks, 2, src, tab, twist, held, *scratch)
    half = 2 * blocks
    for a in range(half):
        early[:, a * LANES : (a + 1) * LANES] = held[a * 8 : (a + 1) * 8, :]
        late[:, a * LANES : (a + 1) * LANES] = held[(half + a) * 8 : (half + a + 1) * 8, :]


def put_ext(ext, i, prev, x):
    ext[i, 6:8, :] = prev[2 * i : 2 * i + 2, :]
    ext[i, 8:, :] = x[...]


def shorted(ext, i, taps, r0, n):
    return (
        taps[i, 0:1, :] * ext[i, 8 + r0 : 8 + r0 + n, :]
        + taps[i, 1:2, :] * ext[i, 7 + r0 : 7 + r0 + n, :]
        + taps[i, 2:3, :] * ext[i, 6 + r0 : 6 + r0 + n, :]
    )


def edge_kernel(q, k, v, go, cs, tails, heads):
    for i, x in enumerate((q, k, v)):
        tails[2 * i : 2 * i + 2, :] = x[6:8, :]
    tails[6:8, :] = jnp.zeros((2, q.shape[1]), f32)
    heads[...] = go[...] * cs[...]


def send_kernel(t_ref, taps, prev, q, k, v, go, fil, out, ext, gof, sems):
    n = q.shape[0]
    copies = [
        pltpu.make_async_copy(src, dst, sems.at[i])
        for i, (src, dst) in enumerate(
            (
                (fil, gof.at[0]),
                (k, ext.at[1, pl.ds(8, n)]),
                (v, ext.at[2, pl.ds(8, n)]),
                (q, ext.at[0, pl.ds(8, n)]),
                (go, gof.at[1]),
            )
        )
    ]
    for c in copies:
        c.start()
    t = t_ref[0]
    for i in range(3):
        ext[i, 6:8, :] = prev[2 * i : 2 * i + 2, :]
    groups = out.shape[0]
    owners = [owner_of(g, t) for g in range(groups)]

    def put(i, r0, piece):
        turned = jnp.transpose(piece)
        for g in range(groups):
            out[owners[g], r0 // LANES, i * 8 : i * 8 + 8, :] = turned[g * 8 : g * 8 + 8]

    starts = range(0, n, LANES)
    copies[0].wait()
    for r0 in starts:
        put(0, r0, gof[0, r0 : r0 + LANES, :])
    copies[1].wait()
    copies[2].wait()
    for r0 in starts:
        put(2, r0, shorted(ext, 1, taps, r0, LANES) * shorted(ext, 2, taps, r0, LANES))
    copies[3].wait()
    copies[4].wait()
    for r0 in starts:
        put(1, r0, gof[1, r0 : r0 + LANES, :] * shorted(ext, 0, taps, r0, LANES))


def side_kernel(
    taps, prev, q, k, v, go, cs, gain, following, zbase, ks, vs, gq, sums, ext, gext
):
    n = q.shape[0]
    for i, x in enumerate((q, k, v)):
        put_ext(ext, i, prev, x)
    gext[n : n + 8, :] = following[...]
    for r0 in range(0, n, LANES):
        gext[r0 : r0 + LANES, :] = go[r0 : r0 + LANES, :] * cs[r0 : r0 + LANES, :]
    totals = [jnp.zeros((1, q.shape[1]), f32) for _ in range(4)]
    for r0 in range(0, n, LANES):
        rows = slice(r0, r0 + LANES)
        gw = go[rows, :] * shorted(ext, 0, taps, r0, LANES)
        k_short = shorted(ext, 1, taps, r0, LANES)
        v_short = shorted(ext, 2, taps, r0, LANES)
        zbase[rows, :] = gain[...] * gw
        ks[rows, :] = k_short
        vs[rows, :] = v_short
        g = gext[rows, :]
        gq[rows, :] = (
            taps[0, 0:1, :] * g
            + taps[0, 1:2, :] * gext[r0 + 1 : r0 + 1 + LANES, :]
            + taps[0, 2:3, :] * gext[r0 + 2 : r0 + 2 + LANES, :]
        )
        for o in range(3):
            totals[o] += jnp.sum(
                g * ext[0, 8 + r0 - o : 8 + r0 - o + LANES, :], axis=0, keepdims=True
            )
        totals[3] += jnp.sum(gw * (k_short * v_short), axis=0, keepdims=True)
    for o in range(4):
        sums[o : o + 1, :] = totals[o]
    sums[4:, :] = jnp.zeros((4, q.shape[1]), f32)


def last_kernel(
    t_ref, corr, zbase, ks, vs, taps, prev, k, v, early, gk, gv, heads, keep, give, ext, gext, held
):
    t = t_ref[0]
    n = k.shape[0]
    groups = corr.shape[0]
    owners = [owner_of(g, t) for g in range(groups)]
    for i, x in enumerate((k, v)):
        ext[i, 6:8, :] = prev[2 * i + 2 : 2 * i + 4, :]
        ext[i, 8:, :] = x[...]
        gext[i, n:, :] = jnp.zeros((8, k.shape[1]), f32)
    totals = [jnp.zeros((1, k.shape[1]), f32) for _ in range(6)]
    for r0 in range(0, n, LANES):
        rows = slice(r0, r0 + LANES)
        for g in range(groups):
            held[g * 8 : g * 8 + 8, :] = corr[owners[g], r0 // LANES]
        grad_z = zbase[rows, :] + jnp.transpose(held[...])
        for i, other in enumerate((vs, ks)):
            g = grad_z * other[rows, :]
            gext[i, rows, :] = g
            for o in range(3):
                totals[i * 3 + o] += jnp.sum(
                    g * ext[i, 8 + r0 - o : 8 + r0 - o + LANES, :], axis=0, keepdims=True
                )
    width = k.shape[1]
    totals = [early[o : o + 1, :] for o in range(4)] + totals
    even = t_ref[1] == 0
    for o in range(5):
        keep[o : o + 1, :] = jnp.where(even, totals[o], totals[5 + o])
        give[o : o + 1, :] = jnp.where(even, totals[5 + o], totals[o])
    for x in (keep, give):
        x[5:8, :] = jnp.zeros((3, width), f32)
    for i, out in enumerate((gk, gv)):
        heads[i] = gext[i, 0:2, :]
        for r0 in range(0, n, LANES):
            out[r0 : r0 + LANES, :] = (
                taps[i + 1, 0:1, :] * gext[i, r0 : r0 + LANES, :]
                + taps[i + 1, 1:2, :] * gext[i, r0 + 1 : r0 + 1 + LANES, :]
                + taps[i + 1, 2:3, :] * gext[i, r0 + 2 : r0 + 2 + LANES, :]
            )


def seam_kernel(gk_in, gv_in, nxt, taps, gk, gv):
    for i, (src, dst) in enumerate(((gk_in, gk), (gv_in, gv))):
        one, two = taps[i + 1, 1:2, :], taps[i + 1, 2:3, :]
        first, second = nxt[i, 0:1, :], nxt[i, 1:2, :]
        dst[...] = src[...]
        dst[6:7, :] = src[6:7, :] + two * first
        dst[7:8, :] = src[7:8, :] + one * first + two * second


def spread_kernel(mine, got, out):
    width = mine.shape[1]
    both = mine[...] + got[...]
    for o in range(5):
        part = both[o : o + 1, :].reshape(1, 1, width)
        out[:, :, o * width : (o + 1) * width] = jnp.broadcast_to(part, (out.shape[0], 1, width))


def gather_kernel(parts, out):
    width = out.shape[1]
    total = parts[0]
    for i in range(1, parts.shape[0]):
        total = total + parts[i]
    for o in range(5):
        out[o : o + 1, :] = total[:, o * width : (o + 1) * width]
    out[5:8, :] = jnp.zeros((3, width), f32)


def finish_kernel(t_ref, mine, other, taps, skip):
    even = t_ref[1] == 0
    rows = [jnp.where(even, mine[o : o + 1, :], other[o : o + 1, :]) for o in range(5)]
    rows += [jnp.where(even, other[o : o + 1, :], mine[o : o + 1, :]) for o in range(5)]
    skip[...] = rows.pop(3)
    for i in range(9):
        taps[i // 3, i % 3 : i % 3 + 1, :] = rows[i]


VM = pl.BlockSpec(memory_space=pltpu.VMEM)
SM = pl.BlockSpec(memory_space=pltpu.SMEM)
HB = pl.BlockSpec(memory_space=pl.ANY)
TB = pl.BlockSpec(memory_space=pltpu.HBM)


def shape(*s):
    return jax.ShapeDtypeStruct(s, f32)


def call(body, ins, outs, args, scratch=(), flops=10**6, nbytes=4 * 10**6):
    return pl.pallas_call(
        body,
        out_shape=outs,
        in_specs=ins,
        out_specs=jax.tree.map(lambda _: VM, outs),
        scratch_shapes=list(scratch),
        cost_estimate=pl.CostEstimate(flops=flops, bytes_accessed=nbytes, transcendentals=0),
        compiler_params=pltpu.CompilerParams(vmem_limit_bytes=40 * 2**20),
    )(*args)


def shifted(value, steps):
    count = lax.axis_size("ctx")
    pairs = [(i, i + steps) for i in range(count) if 0 <= i + steps < count]
    return lax.ppermute(value, "ctx", pairs)


def on_device(q, k, v, taps, fil, gain, cs, go):
    n, width = q.shape
    blocks = lax.axis_size("ctx")
    tp = lax.axis_size("tp")
    seq = n * blocks
    scale = 2.0 / (2 * seq) / math.sqrt(seq)
    tabs = [jnp.asarray(x) for x in tables(blocks, scale)]
    where = [lax.axis_index("tp"), lax.axis_index("ctx") & 1]
    t = jnp.stack([x.astype(jnp.int32) for x in where])

    low = pl.BlockSpec((8, width), lambda i: (n // 8 - 1, 0))
    top = pl.BlockSpec((8, width), lambda i: (0, 0))
    tails, heads = pl.pallas_call(
        edge_kernel,
        grid=(1,),
        out_shape=(shape(8, width), shape(8, width)),
        in_specs=[low, low, low, top, top],
        out_specs=(top, top),
        name="edge",
    )(q, k, v, go, cs)
    prev = shifted(tails, 1)
    nxt_q = shifted(heads, -1)

    ext3 = pltpu.VMEM((3, n + 8, width), f32)
    packed = call(
        send_kernel, [SM, VM, VM] + [HB] * 5, shape(blocks, n // LANES, 24, LANES),
        (t, taps, prev, q, k, v, go, fil),
        [ext3, pltpu.VMEM((2, n, width), f32), pltpu.SemaphoreType.DMA((5,))],
    )
    arrived = lax.all_to_all(packed, "ctx", 0, 0, tiled=True)
    arrived = arrived.reshape(seq // LANES, 24, LANES)
    work = [
        pltpu.VMEM((seq // LANES, 8, LANES), f32),
        pltpu.VMEM((seq // LANES, 8, LANES), f32),
        *(pltpu.VMEM(x.shape, x.dtype) for x in tabs),
        pltpu.SemaphoreType.DMA((4,)),
    ]
    zbase, ks, vs, gq, early = call(
        side_kernel, [VM] * 9,
        (shape(n, width),) * 4 + (shape(8, width),),
        (taps, prev, q, k, v, go, cs, gain.reshape(1, width), nxt_q),
        [ext3, pltpu.VMEM((n + 8, width), f32)],
    )
    corr = call(
        functools.partial(first_kernel, blocks), [HB, TB, TB, HB],
        shape(seq * 8 // LANES, LANES), (arrived, *tabs, early), work,
        flops=2 * 10**9,
    )
    back = lax.all_to_all(corr.reshape(blocks, n // LANES, 8, LANES), "ctx", 0, 0, tiled=True)
    zeta = call(
        functools.partial(second_kernel, blocks), [HB, TB, TB],
        (shape(8, seq // 2), shape(8, seq // 2)), (arrived, *tabs),
        [pltpu.VMEM((seq * 8 // LANES, LANES), f32), *work], flops=2 * 10**9,
    )
    hop_one, hop_two = [], []
    for c in range(blocks):
        for s in range(tp):
            row, column = target_of(c, s)
            hop_one.append((c * tp + s, c * tp + column))
            hop_two.append((c * tp + column, row * tp + column))
    zeta = [lax.ppermute(x, ("ctx", "tp"), hop_one) for x in zeta]
    early_half = lax.ppermute(zeta[0], ("ctx", "tp"), hop_two)
    late_half = lax.ppermute(zeta[1], ("ctx", "tp"), hop_two)
    grad_filter = jnp.concatenate([early_half, late_half], axis=1)

    gk, gv, heads, keep, give = call(
        last_kernel, [SM] + [VM] * 9,
        (shape(n, width), shape(n, width), shape(2, 2, width), shape(8, width), shape(8, width)),
        (t, back, zbase, ks, vs, taps, prev, k, v, early),
        [
            pltpu.VMEM((2, n + 8, width), f32),
            pltpu.VMEM((2, n + 8, width), f32),
            pltpu.VMEM((width, LANES), f32),
        ],
    )
    swap = [(i, i ^ 1) for i in range(blocks)]
    got = lax.ppermute(give, "ctx", swap)
    parts = call(spread_kernel, [VM, VM], shape(blocks // 2, 1, 5 * width), (keep, got))
    same = [list(range(core, blocks, 2)) for core in (0, 1)]
    parts = lax.all_to_all(
        parts, "ctx", 0, 0, axis_index_groups=same, tiled=True
    )
    total = call(gather_kernel, [VM], shape(8, width), (parts,))
    other = lax.ppermute(total, "ctx", swap)
    nxt = shifted(heads, -1)
    gk, gv = pl.pallas_call(
        seam_kernel,
        grid=(1,),
        out_shape=(shape(n, width), shape(n, width)),
        in_specs=[low, low, VM, VM],
        out_specs=(low, low),
        input_output_aliases={0: 0, 1: 1},
        name="seam",
    )(gk, gv, nxt, taps)
    grad_taps, grad_skip = call(
        finish_kernel, [SM, VM, VM], (shape(3, 3, width), shape(1, width)), (t, total, other),
    )
    return gq, gk, gv, grad_filter, grad_taps, grad_skip.reshape(width)


def solution(mesh):
    rows = P("ctx", "tp")
    return jax.shard_map(
        on_device,
        mesh=mesh,
        in_specs=(rows, rows, rows, P(None, None, "tp"), rows, P("tp"), rows, rows),
        out_specs=(rows, rows, rows, P(("ctx", "tp"), None), P(None, None, "tp"), P("tp")),
        check_vma=False,
    )
```

```python
import functools
import math

import jax
import jax.numpy as jnp
import numpy as np
from jax import lax
from jax.experimental import pallas as pl
from jax.experimental.pallas import tpu as pltpu
from jax.sharding import PartitionSpec as P


f32, bf16 = jnp.float32, jnp.bfloat16
LANES = 128


def target_of(c, t):
    x_lo, zp, par, core = c >> 4, (c >> 2) & 3, (c >> 1) & 1, c & 1
    ahead = (t - zp) & 3
    far, kind = ahead >> 1, ahead & 1
    spread = far ^ core ^ (par if kind else 0)
    new_par = far if kind else par ^ far
    across = (t >> 2) ^ x_lo ^ core
    return 4 * t + 2 * new_par + core, across * 4 + kind * 2 + spread


def owner_of(group, t):
    new_par, core, target = group >> 4, (group >> 3) & 1, group & 7
    across, kind, spread = target >> 2, (target >> 1) & 1, target & 1
    far = new_par if kind else spread ^ core
    par = far ^ core ^ spread if kind else new_par ^ far
    zp = (t - (2 * far + kind)) & 3
    x_lo = (t >> 2) ^ across ^ core
    return x_lo * 16 + zp * 4 + par * 2 + core


def halves(table):
    table = np.asarray(table, np.float64).astype(np.float32)
    high = table.astype(bf16)
    low = (table - high.astype(np.float32)).astype(bf16)
    return high, low


@functools.cache
def tables(blocks, scale):
    total = 2 * blocks * 4 * LANES
    rows = np.arange(4 * blocks)
    a = (rows % blocks) * 4 + rows // blocks
    q = np.arange(LANES) + 0.5
    l = np.arange(LANES)
    ang = 2 * np.pi * np.outer(q, a) / (total // LANES)
    outer = np.concatenate([np.cos(ang), -np.sin(ang)], 0)
    back = scale * np.concatenate([np.cos(ang), -np.sin(ang)], 0).T
    ang = 2 * np.pi * np.outer(q, l) / total
    twist_re, twist_im = np.cos(ang).astype(np.float32), -np.sin(ang).astype(np.float32)
    ang = 2 * np.pi * (np.outer(l, l) % LANES) / LANES
    co, si = np.cos(ang), np.sin(ang)
    inner = np.block([[co, -si], [si, co]])
    inner_back = np.block([[co, si], [-si, co]])
    oh, ol = halves(outer)
    bh, bl = halves(back)
    ih, il = halves(inner)
    jh, jl = halves(inner_back)
    ol = np.concatenate([ol[:LANES], ol[LANES:]], 1)
    big = np.concatenate([np.concatenate([oh, oh], 1), ih, il, jh, jl, bh, bl, ol], 0)
    return big, np.concatenate([twist_re, twist_im], 0)


def split(x):
    high = x.astype(bf16)
    return high, (x - high.astype(f32)).astype(bf16)


def mm(a, b):
    return jnp.dot(a, b, preferred_element_type=f32)


def load_pair(src_a, src_b, row_a, row_b, blocks):
    def one(src, row):
        return jnp.concatenate(
            [src[pl.ds(i * 8 + row, blocks, stride=32), :] for i in range(4)], axis=0
        )

    return jnp.concatenate([one(src_a, row_a), one(src_b, row_b)], axis=1)


def forward(pair, tab, twist):
    high, low = split(pair)
    ol = jnp.concatenate([tab[1536:1664, :LANES], tab[1536:1664, LANES:]], axis=0)
    y = mm(tab[0:256, :], jnp.concatenate([high, low], axis=0)) + mm(ol, high)
    re, im = twist[:LANES, :], twist[LANES:, :]
    parts = []
    for s in (0, LANES):
        yr, yi = y[:LANES, s : s + LANES], y[LANES:, s : s + LANES]
        parts.append(jnp.concatenate([yr * re - yi * im, yr * im + yi * re], axis=1))
    high, low = split(jnp.concatenate(parts, axis=0))
    ih, il = tab[256:512, :], tab[512:768, :]
    return mm(high, ih) + mm(low, ih) + mm(high, il)


def conj_times(f, g):
    fr, fi, gr, gi = f[:, :LANES], f[:, LANES:], g[:, :LANES], g[:, LANES:]
    return jnp.concatenate([fr * gr + fi * gi, fr * gi - fi * gr], axis=1)


def backward(pa, pb, tab, twist):
    high, low = split(jnp.concatenate([pa, pb], axis=0))
    jh, jl = tab[768:1024, :], tab[1024:1280, :]
    v = mm(high, jh) + mm(low, jh) + mm(high, jl)
    re, im = twist[:LANES, :], twist[LANES:, :]
    parts = []
    for s in (0, LANES):
        vr, vi = v[s : s + LANES, :LANES], v[s : s + LANES, LANES:]
        parts.append(jnp.concatenate([vr * re + vi * im, vi * re - vr * im], axis=0))
    high, low = split(jnp.concatenate(parts, axis=1))
    bh, bl = tab[1280:1408, :], tab[1408:1536, :]
    return mm(bh, high) + mm(bh, low) + mm(bl, high)


def correlate(blocks, which, src, tab_in, twist_in, out, left, right, tab, twist, sems):
    pairs = (
        (src.at[:, pl.ds(8 * which, 8)], left),
        (src.at[:, pl.ds(8, 8)], right),
        (tab_in, tab),
        (twist_in, twist),
    )
    copies = [pltpu.make_async_copy(x, y, sems.at[i]) for i, (x, y) in enumerate(pairs)]
    for c in copies:
        c.start()
    for c in copies:
        c.wait()
    left, right = (x.reshape(32 * blocks, LANES) for x in (left, right))
    for ch in range(0, 8, 2):
        products = []
        for c in (ch, ch + 1):
            both = forward(load_pair(left, right, c, c, blocks), tab, twist)
            products.append(conj_times(both[:LANES], both[LANES:]))
        corr = backward(*products, tab, twist)
        for s in (0, 1):
            for i in range(4):
                out[pl.ds(i * 8 + ch + s, blocks, stride=32), :] = corr[
                    i * blocks : (i + 1) * blocks, s * LANES : (s + 1) * LANES
                ]


def first_kernel(blocks, src, tab, twist, ahead, out, *scratch):
    correlate(blocks, 0, src, tab, twist, out, *scratch)


def second_kernel(blocks, src, tab, twist, out, held, *scratch):
    correlate(blocks, 2, src, tab, twist, held, *scratch)
    for a in range(4 * blocks):
        out[:, a * LANES : (a + 1) * LANES] = held[a * 8 : (a + 1) * 8, :]


def put_ext(ext, i, prev, x):
    ext[i, 6:8, :] = prev[2 * i : 2 * i + 2, :]
    ext[i, 8:, :] = x[...]


def shorted(ext, i, taps, r0, n):
    return (
        taps[i, 0:1, :] * ext[i, 8 + r0 : 8 + r0 + n, :]
        + taps[i, 1:2, :] * ext[i, 7 + r0 : 7 + r0 + n, :]
        + taps[i, 2:3, :] * ext[i, 6 + r0 : 6 + r0 + n, :]
    )


def edge_kernel(q, k, v, tails):
    for i, x in enumerate((q, k, v)):
        tails[2 * i : 2 * i + 2, :] = x[6:8, :]
    tails[6:8, :] = jnp.zeros((2, q.shape[1]), f32)


def send_kernel(t_ref, taps, prev_in, q, k, v, go, fil, out, ext, gof, prev, sems):
    n = q.shape[0]
    copies = [
        pltpu.make_async_copy(src, dst, sems.at[i])
        for i, (src, dst) in enumerate(
            (
                (fil, gof.at[0]),
                (k, ext.at[1, pl.ds(8, n)]),
                (v, ext.at[2, pl.ds(8, n)]),
                (q, ext.at[0, pl.ds(8, n)]),
                (go, gof.at[1]),
                (prev_in, prev),
            )
        )
    ]
    for c in copies:
        c.start()
    t = t_ref[0]
    groups = out.shape[0]
    owners = [owner_of(g, t) for g in range(groups)]

    def put(i, r0, piece):
        turned = jnp.transpose(piece)
        for g in range(groups):
            out[owners[g], r0 // LANES, i * 8 : i * 8 + 8, :] = turned[g * 8 : g * 8 + 8]

    starts = range(0, n, LANES)
    copies[0].wait()
    for r0 in starts:
        put(0, r0, gof[0, r0 : r0 + LANES, :])
    copies[5].wait()
    for i in range(3):
        ext[i, 6:8, :] = prev[2 * i : 2 * i + 2, :]
    copies[1].wait()
    copies[2].wait()
    for r0 in starts:
        put(2, r0, shorted(ext, 1, taps, r0, LANES) * shorted(ext, 2, taps, r0, LANES))
    copies[3].wait()
    copies[4].wait()
    for r0 in starts:
        put(1, r0, gof[1, r0 : r0 + LANES, :] * shorted(ext, 0, taps, r0, LANES))


def side_kernel(
    taps, prev, q, k, v, go, cs, gain, zbase, ks, vs, gq, sums, ext, gext
):
    n = q.shape[0]
    for i, x in enumerate((q, k, v)):
        put_ext(ext, i, prev, x)
    gext[n:, :] = jnp.zeros((8, q.shape[1]), f32)
    for r0 in range(0, n, LANES):
        gext[r0 : r0 + LANES, :] = go[r0 : r0 + LANES, :] * cs[r0 : r0 + LANES, :]
    totals = [jnp.zeros((1, q.shape[1]), f32) for _ in range(4)]
    for r0 in range(0, n, LANES):
        rows = slice(r0, r0 + LANES)
        gw = go[rows, :] * shorted(ext, 0, taps, r0, LANES)
        k_short = shorted(ext, 1, taps, r0, LANES)
        v_short = shorted(ext, 2, taps, r0, LANES)
        zbase[rows, :] = gain[...] * gw
        ks[rows, :] = k_short
        vs[rows, :] = v_short
        g = gext[rows, :]
        gq[rows, :] = (
            taps[0, 0:1, :] * g
            + taps[0, 1:2, :] * gext[r0 + 1 : r0 + 1 + LANES, :]
            + taps[0, 2:3, :] * gext[r0 + 2 : r0 + 2 + LANES, :]
        )
        for o in range(3):
            totals[o] += jnp.sum(
                g * ext[0, 8 + r0 - o : 8 + r0 - o + LANES, :], axis=0, keepdims=True
            )
        totals[3] += jnp.sum(gw * (k_short * v_short), axis=0, keepdims=True)
    for o in range(4):
        sums[o : o + 1, :] = totals[o]
    sums[4:6, :] = gext[0:2, :]
    sums[6:8, :] = jnp.zeros((2, q.shape[1]), f32)


def last_kernel(
    t_ref, corr, zbase_in, ks_in, vs_in, taps, prev, k, v, early,
    gk, gv, heads, keep, give, ext, gext, held, base, sems,
):
    t = t_ref[0]
    n = k.shape[0]
    steps = []
    for j, r0 in enumerate(range(0, n, LANES)):
        rows = pl.ds(r0, LANES)
        pairs = [(x.at[rows], base.at[i, rows]) for i, x in enumerate((zbase_in, ks_in, vs_in))]
        pairs += [
            (x.at[rows], ext.at[i, pl.ds(8 + r0, LANES)]) for i, x in enumerate((k, v))
        ]
        steps.append(
            [pltpu.make_async_copy(x, y, sems.at[5 * j + i]) for i, (x, y) in enumerate(pairs)]
        )
    for step in steps:
        for c in step:
            c.start()
    zbase, ks, vs = base.at[0], base.at[1], base.at[2]
    groups = corr.shape[0]
    owners = [owner_of(g, t) for g in range(groups)]
    for i in range(2):
        ext[i, 6:8, :] = prev[2 * i + 2 : 2 * i + 4, :]
        gext[i, n:, :] = jnp.zeros((8, k.shape[1]), f32)
    totals = [jnp.zeros((1, k.shape[1]), f32) for _ in range(6)]
    for r0 in range(0, n, LANES):
        rows = slice(r0, r0 + LANES)
        for g in range(groups):
            held[g * 8 : g * 8 + 8, :] = corr[owners[g], r0 // LANES]
        for c in steps[r0 // LANES]:
            c.wait()
        grad_z = zbase[rows, :] + jnp.transpose(held[...])
        for i, other in enumerate((vs, ks)):
            g = grad_z * other[rows, :]
            gext[i, rows, :] = g
            for o in range(3):
                totals[i * 3 + o] += jnp.sum(
                    g * ext[i, 8 + r0 - o : 8 + r0 - o + LANES, :], axis=0, keepdims=True
                )
    width = k.shape[1]
    totals = [early[o : o + 1, :] for o in range(4)] + totals
    even = t_ref[1] == 0
    for o in range(5):
        keep[o : o + 1, :] = jnp.where(even, totals[o], totals[5 + o])
        give[o : o + 1, :] = jnp.where(even, totals[5 + o], totals[o])
    for x in (keep, give):
        x[5:8, :] = jnp.zeros((3, width), f32)
    heads[0:2, :] = early[4:6, :]
    heads[6:8, :] = jnp.zeros((2, width), f32)
    for i, out in enumerate((gk, gv)):
        heads[2 * i + 2 : 2 * i + 4, :] = gext[i, 0:2, :]
        for r0 in range(0, n, LANES):
            out[r0 : r0 + LANES, :] = (
                taps[i + 1, 0:1, :] * gext[i, r0 : r0 + LANES, :]
                + taps[i + 1, 1:2, :] * gext[i, r0 + 1 : r0 + 1 + LANES, :]
                + taps[i + 1, 2:3, :] * gext[i, r0 + 2 : r0 + 2 + LANES, :]
            )


def seam_kernel(gq_in, gk_in, gv_in, nxt, taps, gq, gk, gv):
    for i, (src, dst) in enumerate(((gq_in, gq), (gk_in, gk), (gv_in, gv))):
        one, two = taps[i, 1:2, :], taps[i, 2:3, :]
        first, second = nxt[2 * i : 2 * i + 1, :], nxt[2 * i + 1 : 2 * i + 2, :]
        dst[...] = src[...]
        dst[6:7, :] = src[6:7, :] + two * first
        dst[7:8, :] = src[7:8, :] + one * first + two * second


def spread_kernel(mine, got, out):
    width = mine.shape[1]
    both = mine[...] + got[...]
    for o in range(5):
        part = both[o : o + 1, :].reshape(1, 1, width)
        out[:, :, o * width : (o + 1) * width] = jnp.broadcast_to(part, (out.shape[0], 1, width))


def gather_kernel(parts, out):
    width = out.shape[1]
    total = parts[0]
    for i in range(1, parts.shape[0]):
        total = total + parts[i]
    for o in range(5):
        out[o : o + 1, :] = total[:, o * width : (o + 1) * width]
    out[5:8, :] = jnp.zeros((3, width), f32)


def finish_kernel(t_ref, mine, other, taps, skip):
    even = t_ref[1] == 0
    rows = [jnp.where(even, mine[o : o + 1, :], other[o : o + 1, :]) for o in range(5)]
    rows += [jnp.where(even, other[o : o + 1, :], mine[o : o + 1, :]) for o in range(5)]
    skip[...] = rows.pop(3)
    for i in range(9):
        taps[i // 3, i % 3 : i % 3 + 1, :] = rows[i]


VM = pl.BlockSpec(memory_space=pltpu.VMEM)
SM = pl.BlockSpec(memory_space=pltpu.SMEM)
HB = pl.BlockSpec(memory_space=pl.ANY)
TB = pl.BlockSpec(memory_space=pltpu.HBM)


def shape(*s):
    return jax.ShapeDtypeStruct(s, f32)


def call(body, ins, outs, args, scratch=(), flops=10**6, nbytes=4 * 10**6, room=40):
    return pl.pallas_call(
        body,
        out_shape=outs,
        in_specs=ins,
        out_specs=jax.tree.map(lambda _: VM, outs),
        scratch_shapes=list(scratch),
        cost_estimate=pl.CostEstimate(flops=flops, bytes_accessed=nbytes, transcendentals=0),
        compiler_params=pltpu.CompilerParams(vmem_limit_bytes=room * 2**20),
    )(*args)


def shifted(value, steps):
    count = lax.axis_size("ctx")
    pairs = [(i, i + steps) for i in range(count) if 0 <= i + steps < count]
    return lax.ppermute(value, "ctx", pairs)


def on_device(q, k, v, taps, fil, gain, cs, go):
    n, width = q.shape
    blocks = lax.axis_size("ctx")
    tp = lax.axis_size("tp")
    seq = n * blocks
    scale = 2.0 / (2 * seq) / math.sqrt(seq)
    tabs = [jnp.asarray(x) for x in tables(blocks, scale)]
    where = [lax.axis_index("tp"), lax.axis_index("ctx") & 1]
    t = jnp.stack([x.astype(jnp.int32) for x in where])

    low = pl.BlockSpec((8, width), lambda i: (n // 8 - 1, 0))
    top = pl.BlockSpec((8, width), lambda i: (0, 0))
    tails = pl.pallas_call(
        edge_kernel,
        grid=(1,),
        out_shape=shape(8, width),
        in_specs=[low, low, low],
        out_specs=top,
        name="edge",
    )(q, k, v)
    prev = shifted(tails, 1)

    ext3 = pltpu.VMEM((3, n + 8, width), f32)
    packed = call(
        send_kernel, [SM, VM] + [HB] * 6, shape(blocks, n // LANES, 24, LANES),
        (t, taps, prev, q, k, v, go, fil),
        [
            ext3, pltpu.VMEM((2, n, width), f32), pltpu.VMEM((8, width), f32),
            pltpu.SemaphoreType.DMA((6,)),
        ], room=62,
    )
    arrived = lax.all_to_all(packed, "ctx", 0, 0, tiled=True)
    arrived = arrived.reshape(seq // LANES, 24, LANES)
    work = [
        pltpu.VMEM((seq // LANES, 8, LANES), f32),
        pltpu.VMEM((seq // LANES, 8, LANES), f32),
        *(pltpu.VMEM(x.shape, x.dtype) for x in tabs),
        pltpu.SemaphoreType.DMA((4,)),
    ]
    zbase, ks, vs, gq, early = call(
        side_kernel, [VM] * 8,
        (shape(n, width),) * 4 + (shape(8, width),),
        (taps, prev, q, k, v, go, cs, gain.reshape(1, width)),
        [ext3, pltpu.VMEM((n + 8, width), f32)],
    )
    corr = call(
        functools.partial(first_kernel, blocks), [HB, TB, TB, HB],
        shape(seq * 8 // LANES, LANES), (arrived, *tabs, early), work,
        flops=2 * 10**9, room=62,
    )
    back = lax.all_to_all(corr.reshape(blocks, n // LANES, 8, LANES), "ctx", 0, 0, tiled=True)
    zeta = call(
        functools.partial(second_kernel, blocks), [HB, TB, TB],
        shape(8, seq), (arrived, *tabs),
        [pltpu.VMEM((seq * 8 // LANES, LANES), f32), *work], flops=2 * 10**9, room=62,
    )
    hop_one, hop_two = [], []
    for c in range(blocks):
        for s in range(tp):
            row, column = target_of(c, s)
            hop_one.append((c * tp + s, c * tp + column))
            hop_two.append((c * tp + column, row * tp + column))
    zeta = lax.ppermute(zeta, ("ctx", "tp"), hop_one)
    grad_filter = lax.ppermute(zeta, ("ctx", "tp"), hop_two)

    gk, gv, heads, keep, give = call(
        last_kernel, [SM, VM, HB, HB, HB, VM, VM, HB, HB, VM],
        (shape(n, width), shape(n, width), shape(8, width), shape(8, width), shape(8, width)),
        (t, back, zbase, ks, vs, taps, prev, k, v, early),
        [
            pltpu.VMEM((2, n + 8, width), f32),
            pltpu.VMEM((2, n + 8, width), f32),
            pltpu.VMEM((width, LANES), f32),
            pltpu.VMEM((3, n, width), f32),
            pltpu.SemaphoreType.DMA((5 * (n // LANES),)),
        ], room=60,
    )
    swap = [(i, i ^ 1) for i in range(blocks)]
    got = lax.ppermute(give, "ctx", swap)
    parts = call(spread_kernel, [VM, VM], shape(blocks // 2, 1, 5 * width), (keep, got))
    same = [list(range(core, blocks, 2)) for core in (0, 1)]
    parts = lax.all_to_all(
        parts, "ctx", 0, 0, axis_index_groups=same, tiled=True
    )
    total = call(gather_kernel, [VM], shape(8, width), (parts,))
    other = lax.ppermute(total, "ctx", swap)
    nxt = shifted(heads, -1)
    gq, gk, gv = pl.pallas_call(
        seam_kernel,
        grid=(1,),
        out_shape=(shape(n, width),) * 3,
        in_specs=[low, low, low, VM, VM],
        out_specs=(low, low, low),
        input_output_aliases={0: 0, 1: 1, 2: 2},
        name="seam",
    )(gq, gk, gv, nxt, taps)
    grad_taps, grad_skip = call(
        finish_kernel, [SM, VM, VM], (shape(3, 3, width), shape(1, width)), (t, total, other),
    )
    return gq, gk, gv, grad_filter, grad_taps, grad_skip.reshape(width)


def solution(mesh):
    rows = P("ctx", "tp")
    return jax.shard_map(
        on_device,
        mesh=mesh,
        in_specs=(rows, rows, rows, P(None, None, "tp"), rows, P("tp"), rows, rows),
        out_specs=(rows, rows, rows, P(("ctx", "tp"), None), P(None, None, "tp"), P("tp")),
        check_vma=False,
    )
```

```python
import functools
import math

import jax
import jax.numpy as jnp
import numpy as np
from jax import lax
from jax.experimental import pallas as pl
from jax.experimental.pallas import tpu as pltpu
from jax.sharding import PartitionSpec as P


f32, bf16 = jnp.float32, jnp.bfloat16
LANES = 128


def target_of(c, t):
    x_lo, zp, par, core = c >> 4, (c >> 2) & 3, (c >> 1) & 1, c & 1
    ahead = (t - zp) & 3
    far, kind = ahead >> 1, ahead & 1
    spread = far ^ core ^ (par if kind else 0)
    new_par = far if kind else par ^ far
    across = (t >> 2) ^ x_lo ^ core
    return 4 * t + 2 * new_par + core, across * 4 + kind * 2 + spread


def owner_of(group, t):
    new_par, core, target = group >> 4, (group >> 3) & 1, group & 7
    across, kind, spread = target >> 2, (target >> 1) & 1, target & 1
    far = new_par if kind else spread ^ core
    par = far ^ core ^ spread if kind else new_par ^ far
    zp = (t - (2 * far + kind)) & 3
    x_lo = (t >> 2) ^ across ^ core
    return x_lo * 16 + zp * 4 + par * 2 + core


def halves(table):
    table = np.asarray(table, np.float64).astype(np.float32)
    high = table.astype(bf16)
    low = (table - high.astype(np.float32)).astype(bf16)
    return high, low


@functools.cache
def tables(blocks, scale):
    total = 2 * blocks * 4 * LANES
    rows = np.arange(4 * blocks)
    a = (rows % blocks) * 4 + rows // blocks
    q = np.arange(LANES) + 0.5
    l = np.arange(LANES)
    ang = 2 * np.pi * np.outer(q, a) / (total // LANES)
    outer = np.concatenate([np.cos(ang), -np.sin(ang)], 0)
    back = scale * np.concatenate([np.cos(ang), -np.sin(ang)], 0).T
    ang = 2 * np.pi * np.outer(q, l) / total
    twist_re, twist_im = np.cos(ang).astype(np.float32), -np.sin(ang).astype(np.float32)
    ang = 2 * np.pi * (np.outer(l, l) % LANES) / LANES
    co, si = np.cos(ang), np.sin(ang)
    inner = np.block([[co, -si], [si, co]])
    inner_back = np.block([[co, si], [-si, co]])
    oh, ol = halves(outer)
    bh, bl = halves(back)
    ih, il = halves(inner)
    jh, jl = halves(inner_back)
    ol = np.concatenate([ol[:LANES], ol[LANES:]], 1)
    big = np.concatenate([np.concatenate([oh, oh], 1), ih, il, jh, jl, bh, bl, ol], 0)
    return big, np.concatenate([twist_re, twist_im], 0)


def split(x):
    high = x.astype(bf16)
    return high, (x - high.astype(f32)).astype(bf16)


def mm(a, b):
    return jnp.dot(a, b, preferred_element_type=f32)


def load_pair(src_a, src_b, row_a, row_b, blocks):
    def one(src, row):
        return jnp.concatenate(
            [src[pl.ds(i * 8 + row, blocks, stride=32), :] for i in range(4)], axis=0
        )

    return jnp.concatenate([one(src_a, row_a), one(src_b, row_b)], axis=1)


def forward(pair, tab, twist):
    high, low = split(pair)
    ol = jnp.concatenate([tab[1536:1664, :LANES], tab[1536:1664, LANES:]], axis=0)
    y = mm(tab[0:256, :], jnp.concatenate([high, low], axis=0)) + mm(ol, high)
    re, im = twist[:LANES, :], twist[LANES:, :]
    parts = []
    for s in (0, LANES):
        yr, yi = y[:LANES, s : s + LANES], y[LANES:, s : s + LANES]
        parts.append(jnp.concatenate([yr * re - yi * im, yr * im + yi * re], axis=1))
    high, low = split(jnp.concatenate(parts, axis=0))
    ih, il = tab[256:512, :], tab[512:768, :]
    return mm(high, ih) + mm(low, ih) + mm(high, il)


def conj_times(f, g):
    fr, fi, gr, gi = f[:, :LANES], f[:, LANES:], g[:, :LANES], g[:, LANES:]
    return jnp.concatenate([fr * gr + fi * gi, fr * gi - fi * gr], axis=1)


def backward(pa, pb, tab, twist):
    high, low = split(jnp.concatenate([pa, pb], axis=0))
    jh, jl = tab[768:1024, :], tab[1024:1280, :]
    v = mm(high, jh) + mm(low, jh) + mm(high, jl)
    re, im = twist[:LANES, :], twist[LANES:, :]
    parts = []
    for s in (0, LANES):
        vr, vi = v[s : s + LANES, :LANES], v[s : s + LANES, LANES:]
        parts.append(jnp.concatenate([vr * re + vi * im, vi * re - vr * im], axis=0))
    high, low = split(jnp.concatenate(parts, axis=1))
    bh, bl = tab[1280:1408, :], tab[1408:1536, :]
    return mm(bh, high) + mm(bh, low) + mm(bl, high)


def correlate(blocks, left_in, src, tab_in, twist_in, out, left, right, tab, twist, sems):
    pairs = (
        (left_in.at[:, pl.ds(0, 8)], left),
        (src.at[:, pl.ds(8, 8)], right),
        (tab_in, tab),
        (twist_in, twist),
    )
    copies = [pltpu.make_async_copy(x, y, sems.at[i]) for i, (x, y) in enumerate(pairs)]
    for c in copies:
        c.start()
    for c in copies:
        c.wait()
    left, right = (x.reshape(32 * blocks, LANES) for x in (left, right))
    for ch in range(0, 8, 2):
        products = []
        for c in (ch, ch + 1):
            both = forward(load_pair(left, right, c, c, blocks), tab, twist)
            products.append(conj_times(both[:LANES], both[LANES:]))
        corr = backward(*products, tab, twist)
        for s in (0, 1):
            for i in range(4):
                out[pl.ds(i * 8 + ch + s, blocks, stride=32), :] = corr[
                    i * blocks : (i + 1) * blocks, s * LANES : (s + 1) * LANES
                ]


def first_kernel(blocks, src, tab, twist, ahead, out, *scratch):
    correlate(blocks, src, src, tab, twist, out, *scratch)


def second_kernel(blocks, kv, src, tab, twist, out, held, *scratch):
    correlate(blocks, kv, src, tab, twist, held, *scratch)
    for a in range(4 * blocks):
        out[:, a * LANES : (a + 1) * LANES] = held[a * 8 : (a + 1) * 8, :]


def put_ext(ext, i, prev, x):
    ext[i, 6:8, :] = prev[2 * i : 2 * i + 2, :]
    ext[i, 8:, :] = x[...]


def shorted(ext, i, taps, r0, n):
    return (
        taps[i, 0:1, :] * ext[i, 8 + r0 : 8 + r0 + n, :]
        + taps[i, 1:2, :] * ext[i, 7 + r0 : 7 + r0 + n, :]
        + taps[i, 2:3, :] * ext[i, 6 + r0 : 6 + r0 + n, :]
    )


def edge_kernel(q, k, v, go, fil, tails):
    for i, x in enumerate((q, k, v)):
        tails[2 * i : 2 * i + 2, :] = x[6:8, :]
    tails[6:8, :] = jnp.zeros((2, q.shape[1]), f32)


def send_kernel(t_ref, taps, prev, q, k, v, go, fil, out, late, ext, gof, sems):
    n = q.shape[0]
    copies = [
        pltpu.make_async_copy(src, dst, sems.at[i])
        for i, (src, dst) in enumerate(
            (
                (fil, gof.at[0]),
                (k, ext.at[1, pl.ds(8, n)]),
                (v, ext.at[2, pl.ds(8, n)]),
                (q, ext.at[0, pl.ds(8, n)]),
                (go, gof.at[1]),
            )
        )
    ]
    for c in copies:
        c.start()
    t = t_ref[0]
    for i in range(3):
        ext[i, 6:8, :] = prev[2 * i : 2 * i + 2, :]
    groups = out.shape[0]
    owners = [owner_of(g, t) for g in range(groups)]

    def put(i, r0, piece):
        turned = jnp.transpose(piece)
        at, dst = (0, late) if i == 2 else (i * 8, out)
        for g in range(groups):
            dst[owners[g], r0 // LANES, at : at + 8, :] = turned[g * 8 : g * 8 + 8]

    starts = range(0, n, LANES)
    copies[0].wait()
    for r0 in starts:
        put(0, r0, gof[0, r0 : r0 + LANES, :])
    copies[1].wait()
    copies[2].wait()
    for r0 in starts:
        put(2, r0, shorted(ext, 1, taps, r0, LANES) * shorted(ext, 2, taps, r0, LANES))
    copies[3].wait()
    copies[4].wait()
    for r0 in starts:
        put(1, r0, gof[1, r0 : r0 + LANES, :] * shorted(ext, 0, taps, r0, LANES))


def side_kernel(
    taps, prev, q, k, v, go, cs, gain, zbase, ks, vs, gq, sums, ext, gext
):
    n = q.shape[0]
    for i, x in enumerate((q, k, v)):
        put_ext(ext, i, prev, x)
    gext[n:, :] = jnp.zeros((8, q.shape[1]), f32)
    for r0 in range(0, n, LANES):
        gext[r0 : r0 + LANES, :] = go[r0 : r0 + LANES, :] * cs[r0 : r0 + LANES, :]
    totals = [jnp.zeros((1, q.shape[1]), f32) for _ in range(4)]
    for r0 in range(0, n, LANES):
        rows = slice(r0, r0 + LANES)
        gw = go[rows, :] * shorted(ext, 0, taps, r0, LANES)
        k_short = shorted(ext, 1, taps, r0, LANES)
        v_short = shorted(ext, 2, taps, r0, LANES)
        zbase[rows, :] = gain[...] * gw
        ks[rows, :] = k_short
        vs[rows, :] = v_short
        g = gext[rows, :]
        gq[rows, :] = (
            taps[0, 0:1, :] * g
            + taps[0, 1:2, :] * gext[r0 + 1 : r0 + 1 + LANES, :]
            + taps[0, 2:3, :] * gext[r0 + 2 : r0 + 2 + LANES, :]
        )
        for o in range(3):
            totals[o] += jnp.sum(
                g * ext[0, 8 + r0 - o : 8 + r0 - o + LANES, :], axis=0, keepdims=True
            )
        totals[3] += jnp.sum(gw * (k_short * v_short), axis=0, keepdims=True)
    for o in range(4):
        sums[o : o + 1, :] = totals[o]
    sums[4:6, :] = gext[0:2, :]
    sums[6:8, :] = jnp.zeros((2, q.shape[1]), f32)


def last_kernel(
    t_ref, corr, zbase, ks, vs, taps, prev, k, v, early, gk, gv, heads, keep, give, ext, gext, held
):
    t = t_ref[0]
    n = k.shape[0]
    groups = corr.shape[0]
    owners = [owner_of(g, t) for g in range(groups)]
    for i, x in enumerate((k, v)):
        ext[i, 6:8, :] = prev[2 * i + 2 : 2 * i + 4, :]
        ext[i, 8:, :] = x[...]
        gext[i, n:, :] = jnp.zeros((8, k.shape[1]), f32)
    totals = [jnp.zeros((1, k.shape[1]), f32) for _ in range(6)]
    for r0 in range(0, n, LANES):
        rows = slice(r0, r0 + LANES)
        for g in range(groups):
            held[g * 8 : g * 8 + 8, :] = corr[owners[g], r0 // LANES]
        grad_z = zbase[rows, :] + jnp.transpose(held[...])
        for i, other in enumerate((vs, ks)):
            g = grad_z * other[rows, :]
            gext[i, rows, :] = g
            for o in range(3):
                totals[i * 3 + o] += jnp.sum(
                    g * ext[i, 8 + r0 - o : 8 + r0 - o + LANES, :], axis=0, keepdims=True
                )
    width = k.shape[1]
    totals = [early[o : o + 1, :] for o in range(4)] + totals
    even = t_ref[1] == 0
    for o in range(5):
        keep[o : o + 1, :] = jnp.where(even, totals[o], totals[5 + o])
        give[o : o + 1, :] = jnp.where(even, totals[5 + o], totals[o])
    for x in (keep, give):
        x[5:8, :] = jnp.zeros((3, width), f32)
    heads[0:2, :] = early[4:6, :]
    heads[6:8, :] = jnp.zeros((2, width), f32)
    for i, out in enumerate((gk, gv)):
        heads[2 * i + 2 : 2 * i + 4, :] = gext[i, 0:2, :]
        for r0 in range(0, n, LANES):
            out[r0 : r0 + LANES, :] = (
                taps[i + 1, 0:1, :] * gext[i, r0 : r0 + LANES, :]
                + taps[i + 1, 1:2, :] * gext[i, r0 + 1 : r0 + 1 + LANES, :]
                + taps[i + 1, 2:3, :] * gext[i, r0 + 2 : r0 + 2 + LANES, :]
            )


def seam_kernel(gq_in, gk_in, gv_in, nxt, taps, gq, gk, gv):
    for i, (src, dst) in enumerate(((gq_in, gq), (gk_in, gk), (gv_in, gv))):
        one, two = taps[i, 1:2, :], taps[i, 2:3, :]
        first, second = nxt[2 * i : 2 * i + 1, :], nxt[2 * i + 1 : 2 * i + 2, :]
        dst[...] = src[...]
        dst[6:7, :] = src[6:7, :] + two * first
        dst[7:8, :] = src[7:8, :] + one * first + two * second


def spread_kernel(mine, got, out):
    width = mine.shape[1]
    both = mine[...] + got[...]
    for o in range(5):
        part = both[o : o + 1, :].reshape(1, 1, width)
        out[:, :, o * width : (o + 1) * width] = jnp.broadcast_to(part, (out.shape[0], 1, width))


def gather_kernel(parts, out):
    width = out.shape[1]
    total = parts[0]
    for i in range(1, parts.shape[0]):
        total = total + parts[i]
    for o in range(5):
        out[o : o + 1, :] = total[:, o * width : (o + 1) * width]
    out[5:8, :] = jnp.zeros((3, width), f32)


def finish_kernel(t_ref, mine, other, taps, skip):
    even = t_ref[1] == 0
    rows = [jnp.where(even, mine[o : o + 1, :], other[o : o + 1, :]) for o in range(5)]
    rows += [jnp.where(even, other[o : o + 1, :], mine[o : o + 1, :]) for o in range(5)]
    skip[...] = rows.pop(3)
    for i in range(9):
        taps[i // 3, i % 3 : i % 3 + 1, :] = rows[i]


VM = pl.BlockSpec(memory_space=pltpu.VMEM)
SM = pl.BlockSpec(memory_space=pltpu.SMEM)
HB = pl.BlockSpec(memory_space=pl.ANY)
TB = pl.BlockSpec(memory_space=pltpu.HBM)


def shape(*s):
    return jax.ShapeDtypeStruct(s, f32)


def call(body, ins, outs, args, scratch=(), flops=10**6, nbytes=4 * 10**6, room=40):
    return pl.pallas_call(
        body,
        out_shape=outs,
        in_specs=ins,
        out_specs=jax.tree.map(lambda _: VM, outs),
        scratch_shapes=list(scratch),
        cost_estimate=pl.CostEstimate(flops=flops, bytes_accessed=nbytes, transcendentals=0),
        compiler_params=pltpu.CompilerParams(vmem_limit_bytes=room * 2**20),
    )(*args)


def shifted(value, steps):
    count = lax.axis_size("ctx")
    pairs = [(i, i + steps) for i in range(count) if 0 <= i + steps < count]
    return lax.ppermute(value, "ctx", pairs)


def on_device(q, k, v, taps, fil, gain, cs, go):
    n, width = q.shape
    blocks = lax.axis_size("ctx")
    tp = lax.axis_size("tp")
    seq = n * blocks
    scale = 2.0 / (2 * seq) / math.sqrt(seq)
    tabs = [jnp.asarray(x) for x in tables(blocks, scale)]
    where = [lax.axis_index("tp"), lax.axis_index("ctx") & 1]
    t = jnp.stack([x.astype(jnp.int32) for x in where])

    low = pl.BlockSpec((8, width), lambda i: (n // 8 - 1, 0))
    top = pl.BlockSpec((8, width), lambda i: (0, 0))
    tails = pl.pallas_call(
        edge_kernel,
        grid=(1,),
        out_shape=shape(8, width),
        in_specs=[low, low, low, top, top],
        out_specs=top,
        name="edge",
    )(q, k, v, go, fil)
    prev = shifted(tails, 1)

    ext3 = pltpu.VMEM((3, n + 8, width), f32)
    packed, packed_kv = call(
        send_kernel, [SM, VM, VM] + [HB] * 5,
        (shape(blocks, n // LANES, 16, LANES), shape(blocks, n // LANES, 8, LANES)),
        (t, taps, prev, q, k, v, go, fil),
        [ext3, pltpu.VMEM((2, n, width), f32), pltpu.SemaphoreType.DMA((5,))],
    )
    arrived = lax.all_to_all(packed, "ctx", 0, 0, tiled=True)
    arrived_kv = lax.all_to_all(packed_kv, "ctx", 0, 0, tiled=True)
    arrived = arrived.reshape(seq // LANES, 16, LANES)
    arrived_kv = arrived_kv.reshape(seq // LANES, 8, LANES)
    work = [
        pltpu.VMEM((seq // LANES, 8, LANES), f32),
        pltpu.VMEM((seq // LANES, 8, LANES), f32),
        *(pltpu.VMEM(x.shape, x.dtype) for x in tabs),
        pltpu.SemaphoreType.DMA((4,)),
    ]
    zbase, ks, vs, gq, early = call(
        side_kernel, [VM] * 8,
        (shape(n, width),) * 4 + (shape(8, width),),
        (taps, prev, q, k, v, go, cs, gain.reshape(1, width)),
        [ext3, pltpu.VMEM((n + 8, width), f32)],
    )
    corr = call(
        functools.partial(first_kernel, blocks), [HB, TB, TB, HB],
        shape(seq * 8 // LANES, LANES), (arrived, *tabs, early), work,
        flops=2 * 10**9, room=58,
    )
    back = lax.all_to_all(corr.reshape(blocks, n // LANES, 8, LANES), "ctx", 0, 0, tiled=True)
    zeta = call(
        functools.partial(second_kernel, blocks), [HB, HB, TB, TB],
        shape(8, seq), (arrived_kv, arrived, *tabs),
        [pltpu.VMEM((seq * 8 // LANES, LANES), f32), *work], flops=2 * 10**9, room=58,
    )
    hop_one, hop_two = [], []
    for c in range(blocks):
        for s in range(tp):
            row, column = target_of(c, s)
            hop_one.append((c * tp + s, c * tp + column))
            hop_two.append((c * tp + column, row * tp + column))
    zeta = lax.ppermute(zeta, ("ctx", "tp"), hop_one)
    grad_filter = lax.ppermute(zeta, ("ctx", "tp"), hop_two)

    gk, gv, heads, keep, give = call(
        last_kernel, [SM] + [VM] * 9,
        (shape(n, width), shape(n, width), shape(8, width), shape(8, width), shape(8, width)),
        (t, back, zbase, ks, vs, taps, prev, k, v, early),
        [
            pltpu.VMEM((2, n + 8, width), f32),
            pltpu.VMEM((2, n + 8, width), f32),
            pltpu.VMEM((width, LANES), f32),
        ],
    )
    swap = [(i, i ^ 1) for i in range(blocks)]
    got = lax.ppermute(give, "ctx", swap)
    parts = call(spread_kernel, [VM, VM], shape(blocks // 2, 1, 5 * width), (keep, got))
    same = [list(range(core, blocks, 2)) for core in (0, 1)]
    parts = lax.all_to_all(
        parts, "ctx", 0, 0, axis_index_groups=same, tiled=True
    )
    total = call(gather_kernel, [VM], shape(8, width), (parts,))
    other = lax.ppermute(total, "ctx", swap)
    nxt = shifted(heads, -1)
    gq, gk, gv = pl.pallas_call(
        seam_kernel,
        grid=(1,),
        out_shape=(shape(n, width),) * 3,
        in_specs=[low, low, low, VM, VM],
        out_specs=(low, low, low),
        input_output_aliases={0: 0, 1: 1, 2: 2},
        name="seam",
    )(gq, gk, gv, nxt, taps)
    grad_taps, grad_skip = call(
        finish_kernel, [SM, VM, VM], (shape(3, 3, width), shape(1, width)), (t, total, other),
    )
    return gq, gk, gv, grad_filter, grad_taps, grad_skip.reshape(width)


def solution(mesh):
    rows = P("ctx", "tp")
    return jax.shard_map(
        on_device,
        mesh=mesh,
        in_specs=(rows, rows, rows, P(None, None, "tp"), rows, P("tp"), rows, rows),
        out_specs=(rows, rows, rows, P(("ctx", "tp"), None), P(None, None, "tp"), P("tp")),
        check_vma=False,
    )
```

```python
import functools
import math

import jax
import jax.numpy as jnp
import numpy as np
from jax import lax
from jax.experimental import pallas as pl
from jax.experimental.pallas import tpu as pltpu
from jax.sharding import PartitionSpec as P


f32, bf16 = jnp.float32, jnp.bfloat16
LANES = 128


def target_of(c, t):
    x_lo, zp, par, core = c >> 4, (c >> 2) & 3, (c >> 1) & 1, c & 1
    ahead = (t - zp) & 3
    far, kind = ahead >> 1, ahead & 1
    spread = far ^ core ^ (par if kind else 0)
    new_par = far if kind else par ^ far
    across = (t >> 2) ^ x_lo ^ core
    return 4 * t + 2 * new_par + core, across * 4 + kind * 2 + spread


def owner_of(group, t):
    new_par, core, target = group >> 4, (group >> 3) & 1, group & 7
    across, kind, spread = target >> 2, (target >> 1) & 1, target & 1
    far = new_par if kind else spread ^ core
    par = far ^ core ^ spread if kind else new_par ^ far
    zp = (t - (2 * far + kind)) & 3
    x_lo = (t >> 2) ^ across ^ core
    return x_lo * 16 + zp * 4 + par * 2 + core


def halves(table):
    table = np.asarray(table, np.float64).astype(np.float32)
    high = table.astype(bf16)
    low = (table - high.astype(np.float32)).astype(bf16)
    return high, low


@functools.cache
def tables(blocks, scale):
    total = 2 * blocks * 4 * LANES
    rows = np.arange(4 * blocks)
    a = (rows % blocks) * 4 + rows // blocks
    q = np.arange(LANES) + 0.5
    l = np.arange(LANES)
    ang = 2 * np.pi * np.outer(q, a) / (total // LANES)
    outer = np.concatenate([np.cos(ang), -np.sin(ang)], 0)
    back = scale * np.concatenate([np.cos(ang), -np.sin(ang)], 0).T
    ang = 2 * np.pi * np.outer(q, l) / total
    twist_re, twist_im = np.cos(ang).astype(np.float32), -np.sin(ang).astype(np.float32)
    ang = 2 * np.pi * (np.outer(l, l) % LANES) / LANES
    co, si = np.cos(ang), np.sin(ang)
    inner = np.block([[co, -si], [si, co]])
    inner_back = np.block([[co, si], [-si, co]])
    oh, ol = halves(outer)
    bh, bl = halves(back)
    ih, il = halves(inner)
    jh, jl = halves(inner_back)
    ol = np.concatenate([ol[:LANES], ol[LANES:]], 1)
    big = np.concatenate([np.concatenate([oh, oh], 1), ih, il, jh, jl, bh, bl, ol], 0)
    return big, np.concatenate([twist_re, twist_im], 0)


def split(x):
    high = x.astype(bf16)
    return high, (x - high.astype(f32)).astype(bf16)


def mm(a, b):
    return jnp.dot(a, b, preferred_element_type=f32)


def load_pair(src_a, src_b, row_a, row_b, blocks):
    def one(src, row):
        return jnp.concatenate(
            [src[pl.ds(i * 8 + row, blocks, stride=32), :] for i in range(4)], axis=0
        )

    return jnp.concatenate([one(src_a, row_a), one(src_b, row_b)], axis=1)


def forward(pair, tab, twist):
    high, low = split(pair)
    ol = jnp.concatenate([tab[1536:1664, :LANES], tab[1536:1664, LANES:]], axis=0)
    y = mm(tab[0:256, :], jnp.concatenate([high, low], axis=0)) + mm(ol, high)
    re, im = twist[:LANES, :], twist[LANES:, :]
    parts = []
    for s in (0, LANES):
        yr, yi = y[:LANES, s : s + LANES], y[LANES:, s : s + LANES]
        parts.append(jnp.concatenate([yr * re - yi * im, yr * im + yi * re], axis=1))
    high, low = split(jnp.concatenate(parts, axis=0))
    ih, il = tab[256:512, :], tab[512:768, :]
    return mm(high, ih) + mm(low, ih) + mm(high, il)


def conj_times(f, g):
    fr, fi, gr, gi = f[:, :LANES], f[:, LANES:], g[:, :LANES], g[:, LANES:]
    return jnp.concatenate([fr * gr + fi * gi, fr * gi - fi * gr], axis=1)


def backward(pa, pb, tab, twist):
    high, low = split(jnp.concatenate([pa, pb], axis=0))
    jh, jl = tab[768:1024, :], tab[1024:1280, :]
    v = mm(high, jh) + mm(low, jh) + mm(high, jl)
    re, im = twist[:LANES, :], twist[LANES:, :]
    parts = []
    for s in (0, LANES):
        vr, vi = v[s : s + LANES, :LANES], v[s : s + LANES, LANES:]
        parts.append(jnp.concatenate([vr * re + vi * im, vi * re - vr * im], axis=0))
    high, low = split(jnp.concatenate(parts, axis=1))
    bh, bl = tab[1280:1408, :], tab[1408:1536, :]
    return mm(bh, high) + mm(bh, low) + mm(bl, high)


def correlate(blocks, which, src, tab_in, twist_in, out, left, right, tab, twist, sems):
    pairs = (
        (src.at[:, pl.ds(8 * which, 8)], left),
        (src.at[:, pl.ds(8, 8)], right),
        (tab_in, tab),
        (twist_in, twist),
    )
    copies = [pltpu.make_async_copy(x, y, sems.at[i]) for i, (x, y) in enumerate(pairs)]
    for c in copies:
        c.start()
    for c in copies:
        c.wait()
    left, right = (x.reshape(32 * blocks, LANES) for x in (left, right))
    for ch in range(0, 8, 2):
        products = []
        for c in (ch, ch + 1):
            both = forward(load_pair(left, right, c, c, blocks), tab, twist)
            products.append(conj_times(both[:LANES], both[LANES:]))
        corr = backward(*products, tab, twist)
        for s in (0, 1):
            for i in range(4):
                out[pl.ds(i * 8 + ch + s, blocks, stride=32), :] = corr[
                    i * blocks : (i + 1) * blocks, s * LANES : (s + 1) * LANES
                ]


def first_kernel(blocks, src, tab, twist, ahead, out, *scratch):
    correlate(blocks, 0, src, tab, twist, out, *scratch)


def second_kernel(blocks, src, tab, twist, out, held, *scratch):
    correlate(blocks, 2, src, tab, twist, held, *scratch)
    for a in range(4 * blocks):
        out[:, a * LANES : (a + 1) * LANES] = held[a * 8 : (a + 1) * 8, :]


def put_ext(ext, i, prev, x):
    ext[i, 6:8, :] = prev[2 * i : 2 * i + 2, :]
    ext[i, 8:, :] = x[...]


def shorted(ext, i, taps, r0, n):
    return (
        taps[i, 0:1, :] * ext[i, 8 + r0 : 8 + r0 + n, :]
        + taps[i, 1:2, :] * ext[i, 7 + r0 : 7 + r0 + n, :]
        + taps[i, 2:3, :] * ext[i, 6 + r0 : 6 + r0 + n, :]
    )


def edge_kernel(q, k, v, go, fil, tails):
    for i, x in enumerate((q, k, v)):
        tails[2 * i : 2 * i + 2, :] = x[6:8, :]
    tails[6:8, :] = jnp.zeros((2, q.shape[1]), f32)


def send_kernel(t_ref, taps, prev, q, k, v, go, fil, out, ext, gof, sems):
    n = q.shape[0]
    copies = [
        pltpu.make_async_copy(src, dst, sems.at[i])
        for i, (src, dst) in enumerate(
            (
                (fil, gof.at[0]),
                (k, ext.at[1, pl.ds(8, n)]),
                (v, ext.at[2, pl.ds(8, n)]),
                (q, ext.at[0, pl.ds(8, n)]),
                (go, gof.at[1]),
            )
        )
    ]
    for c in copies:
        c.start()
    t = t_ref[0]
    for i in range(3):
        ext[i, 6:8, :] = prev[2 * i : 2 * i + 2, :]
    groups = out.shape[0]
    owners = [owner_of(g, t) for g in range(groups)]

    def put(i, r0, piece):
        turned = jnp.transpose(piece)
        for g in range(groups):
            out[owners[g], r0 // LANES, i * 8 : i * 8 + 8, :] = turned[g * 8 : g * 8 + 8]

    starts = range(0, n, LANES)
    copies[0].wait()
    for r0 in starts:
        put(0, r0, gof[0, r0 : r0 + LANES, :])
    copies[1].wait()
    copies[2].wait()
    for r0 in starts:
        put(2, r0, shorted(ext, 1, taps, r0, LANES) * shorted(ext, 2, taps, r0, LANES))
    copies[3].wait()
    copies[4].wait()
    for r0 in starts:
        put(1, r0, gof[1, r0 : r0 + LANES, :] * shorted(ext, 0, taps, r0, LANES))


def side_kernel(
    taps, prev, q, k, v, go, cs, gain, zbase, ks, vs, gq, sums, ext, gext
):
    n = q.shape[0]
    for i, x in enumerate((q, k, v)):
        put_ext(ext, i, prev, x)
    gext[n:, :] = jnp.zeros((8, q.shape[1]), f32)
    for r0 in range(0, n, LANES):
        gext[r0 : r0 + LANES, :] = go[r0 : r0 + LANES, :] * cs[r0 : r0 + LANES, :]
    totals = [jnp.zeros((1, q.shape[1]), f32) for _ in range(4)]
    for r0 in range(0, n, LANES):
        rows = slice(r0, r0 + LANES)
        gw = go[rows, :] * shorted(ext, 0, taps, r0, LANES)
        k_short = shorted(ext, 1, taps, r0, LANES)
        v_short = shorted(ext, 2, taps, r0, LANES)
        zbase[rows, :] = gain[...] * gw
        ks[rows, :] = k_short
        vs[rows, :] = v_short
        g = gext[rows, :]
        gq[rows, :] = (
            taps[0, 0:1, :] * g
            + taps[0, 1:2, :] * gext[r0 + 1 : r0 + 1 + LANES, :]
            + taps[0, 2:3, :] * gext[r0 + 2 : r0 + 2 + LANES, :]
        )
        for o in range(3):
            totals[o] += jnp.sum(
                g * ext[0, 8 + r0 - o : 8 + r0 - o + LANES, :], axis=0, keepdims=True
            )
        totals[3] += jnp.sum(gw * (k_short * v_short), axis=0, keepdims=True)
    for o in range(4):
        sums[o : o + 1, :] = totals[o]
    sums[4:6, :] = gext[0:2, :]
    sums[6:8, :] = jnp.zeros((2, q.shape[1]), f32)


def last_kernel(
    t_ref, corr, zbase, ks, vs, taps, prev, k, v, early, gk, gv, heads, keep, give, ext, gext, held
):
    t = t_ref[0]
    n = k.shape[0]
    groups = corr.shape[0]
    owners = [owner_of(g, t) for g in range(groups)]
    for i, x in enumerate((k, v)):
        ext[i, 6:8, :] = prev[2 * i + 2 : 2 * i + 4, :]
        ext[i, 8:, :] = x[...]
        gext[i, n:, :] = jnp.zeros((8, k.shape[1]), f32)
    totals = [jnp.zeros((1, k.shape[1]), f32) for _ in range(6)]
    for r0 in range(0, n, LANES):
        rows = slice(r0, r0 + LANES)
        for g in range(groups):
            held[g * 8 : g * 8 + 8, :] = corr[owners[g], r0 // LANES]
        grad_z = zbase[rows, :] + jnp.transpose(held[...])
        for i, other in enumerate((vs, ks)):
            g = grad_z * other[rows, :]
            gext[i, rows, :] = g
            for o in range(3):
                totals[i * 3 + o] += jnp.sum(
                    g * ext[i, 8 + r0 - o : 8 + r0 - o + LANES, :], axis=0, keepdims=True
                )
    width = k.shape[1]
    totals = [early[o : o + 1, :] for o in range(4)] + totals
    even = t_ref[1] == 0
    for o in range(5):
        keep[o : o + 1, :] = jnp.where(even, totals[o], totals[5 + o])
        give[o : o + 1, :] = jnp.where(even, totals[5 + o], totals[o])
    for x in (keep, give):
        x[5:8, :] = jnp.zeros((3, width), f32)
    heads[0:2, :] = early[4:6, :]
    heads[6:8, :] = jnp.zeros((2, width), f32)
    for i, out in enumerate((gk, gv)):
        heads[2 * i + 2 : 2 * i + 4, :] = gext[i, 0:2, :]
        for r0 in range(0, n, LANES):
            out[r0 : r0 + LANES, :] = (
                taps[i + 1, 0:1, :] * gext[i, r0 : r0 + LANES, :]
                + taps[i + 1, 1:2, :] * gext[i, r0 + 1 : r0 + 1 + LANES, :]
                + taps[i + 1, 2:3, :] * gext[i, r0 + 2 : r0 + 2 + LANES, :]
            )


def seam_kernel(gq_in, gk_in, gv_in, nxt, taps, gq, gk, gv):
    for i, (src, dst) in enumerate(((gq_in, gq), (gk_in, gk), (gv_in, gv))):
        one, two = taps[i, 1:2, :], taps[i, 2:3, :]
        first, second = nxt[2 * i : 2 * i + 1, :], nxt[2 * i + 1 : 2 * i + 2, :]
        dst[...] = src[...]
        dst[6:7, :] = src[6:7, :] + two * first
        dst[7:8, :] = src[7:8, :] + one * first + two * second


def spread_kernel(mine, got, out):
    width = mine.shape[1]
    both = mine[...] + got[...]
    for o in range(5):
        part = both[o : o + 1, :].reshape(1, 1, width)
        out[:, :, o * width : (o + 1) * width] = jnp.broadcast_to(part, (out.shape[0], 1, width))


def gather_kernel(parts, out):
    width = out.shape[1]
    total = parts[0]
    for i in range(1, parts.shape[0]):
        total = total + parts[i]
    for o in range(5):
        out[o : o + 1, :] = total[:, o * width : (o + 1) * width]
    out[5:8, :] = jnp.zeros((3, width), f32)


def finish_kernel(t_ref, mine, other, taps, skip):
    even = t_ref[1] == 0
    rows = [jnp.where(even, mine[o : o + 1, :], other[o : o + 1, :]) for o in range(5)]
    rows += [jnp.where(even, other[o : o + 1, :], mine[o : o + 1, :]) for o in range(5)]
    skip[...] = rows.pop(3)
    for i in range(9):
        taps[i // 3, i % 3 : i % 3 + 1, :] = rows[i]


VM = pl.BlockSpec(memory_space=pltpu.VMEM)
SM = pl.BlockSpec(memory_space=pltpu.SMEM)
HB = pl.BlockSpec(memory_space=pl.ANY)
TB = pl.BlockSpec(memory_space=pltpu.HBM)


def shape(*s):
    return jax.ShapeDtypeStruct(s, f32)


def call(body, ins, outs, args, scratch=(), flops=10**6, nbytes=4 * 10**6, room=40):
    return pl.pallas_call(
        body,
        out_shape=outs,
        in_specs=ins,
        out_specs=jax.tree.map(lambda _: VM, outs),
        scratch_shapes=list(scratch),
        cost_estimate=pl.CostEstimate(flops=flops, bytes_accessed=nbytes, transcendentals=0),
        compiler_params=pltpu.CompilerParams(vmem_limit_bytes=room * 2**20),
    )(*args)


def shifted(value, steps):
    count = lax.axis_size("ctx")
    pairs = [(i, i + steps) for i in range(count) if 0 <= i + steps < count]
    return lax.ppermute(value, "ctx", pairs)


def on_device(q, k, v, taps, fil, gain, cs, go):
    n, width = q.shape
    blocks = lax.axis_size("ctx")
    tp = lax.axis_size("tp")
    seq = n * blocks
    scale = 2.0 / (2 * seq) / math.sqrt(seq)
    tabs = [jnp.asarray(x) for x in tables(blocks, scale)]
    where = [lax.axis_index("tp"), lax.axis_index("ctx") & 1]
    t = jnp.stack([x.astype(jnp.int32) for x in where])

    low = pl.BlockSpec((8, width), lambda i: (n // 8 - 1, 0))
    top = pl.BlockSpec((8, width), lambda i: (0, 0))
    tails = pl.pallas_call(
        edge_kernel,
        grid=(1,),
        out_shape=shape(8, width),
        in_specs=[low, low, low, top, top],
        out_specs=top,
        name="edge",
    )(q, k, v, go, fil)
    prev = shifted(tails, 1)

    ext3 = pltpu.VMEM((3, n + 8, width), f32)
    packed = call(
        send_kernel, [SM, VM, VM] + [HB] * 5, shape(blocks, n // LANES, 24, LANES),
        (t, taps, prev, q, k, v, go, fil),
        [ext3, pltpu.VMEM((2, n, width), f32), pltpu.SemaphoreType.DMA((5,))],
    )
    arrived = lax.all_to_all(packed, "ctx", 0, 0, tiled=True)
    arrived = arrived.reshape(seq // LANES, 24, LANES)
    work = [
        pltpu.VMEM((seq // LANES, 8, LANES), f32),
        pltpu.VMEM((seq // LANES, 8, LANES), f32),
        *(pltpu.VMEM(x.shape, x.dtype) for x in tabs),
        pltpu.SemaphoreType.DMA((4,)),
    ]
    zbase, ks, vs, gq, early = call(
        side_kernel, [VM] * 8,
        (shape(n, width),) * 4 + (shape(8, width),),
        (taps, prev, q, k, v, go, cs, gain.reshape(1, width)),
        [ext3, pltpu.VMEM((n + 8, width), f32)],
    )
    corr = call(
        functools.partial(first_kernel, blocks), [HB, TB, TB, HB],
        shape(seq * 8 // LANES, LANES), (arrived, *tabs, early), work,
        flops=2 * 10**9, room=58,
    )
    back = lax.all_to_all(corr.reshape(blocks, n // LANES, 8, LANES), "ctx", 0, 0, tiled=True)
    zeta = call(
        functools.partial(second_kernel, blocks), [HB, TB, TB],
        shape(8, seq), (arrived, *tabs),
        [pltpu.VMEM((seq * 8 // LANES, LANES), f32), *work], flops=2 * 10**9, room=58,
    )
    hop_one, hop_two = [], []
    for c in range(blocks):
        for s in range(tp):
            row, column = target_of(c, s)
            hop_one.append((c * tp + s, c * tp + column))
            hop_two.append((c * tp + column, row * tp + column))
    zeta = lax.ppermute(zeta, ("ctx", "tp"), hop_one)
    grad_filter = lax.ppermute(zeta, ("ctx", "tp"), hop_two)

    gk, gv, heads, keep, give = call(
        last_kernel, [SM] + [VM] * 9,
        (shape(n, width), shape(n, width), shape(8, width), shape(8, width), shape(8, width)),
        (t, back, zbase, ks, vs, taps, prev, k, v, early),
        [
            pltpu.VMEM((2, n + 8, width), f32),
            pltpu.VMEM((2, n + 8, width), f32),
            pltpu.VMEM((width, LANES), f32),
        ],
    )
    swap = [(i, i ^ 1) for i in range(blocks)]
    got = lax.ppermute(give, "ctx", swap)
    parts = call(spread_kernel, [VM, VM], shape(blocks // 2, 1, 5 * width), (keep, got))
    same = [list(range(core, blocks, 2)) for core in (0, 1)]
    parts = lax.all_to_all(
        parts, "ctx", 0, 0, axis_index_groups=same, tiled=True
    )
    total = call(gather_kernel, [VM], shape(8, width), (parts,))
    other = lax.ppermute(total, "ctx", swap)
    nxt = shifted(heads, -1)
    gq, gk, gv = pl.pallas_call(
        seam_kernel,
        grid=(1,),
        out_shape=(shape(n, width),) * 3,
        in_specs=[low, low, low, VM, VM],
        out_specs=(low, low, low),
        input_output_aliases={0: 0, 1: 1, 2: 2},
        name="seam",
    )(gq, gk, gv, nxt, taps)
    grad_taps, grad_skip = call(
        finish_kernel, [SM, VM, VM], (shape(3, 3, width), shape(1, width)), (t, total, other),
    )
    return gq, gk, gv, grad_filter, grad_taps, grad_skip.reshape(width)


def solution(mesh):
    rows = P("ctx", "tp")
    return jax.shard_map(
        on_device,
        mesh=mesh,
        in_specs=(rows, rows, rows, P(None, None, "tp"), rows, P("tp"), rows, rows),
        out_specs=(rows, rows, rows, P(("ctx", "tp"), None), P(None, None, "tp"), P("tp")),
        check_vma=False,
    )
```
